32 devices in a mesh: dp: 8 (over z, y), tensor: 4 (over x, core).
Axes of the slice: x: 2, y: 2, z: 4, core: 2. Of those that a mesh axis runs over, the one named last changes fastest.
Arguments:
- tokens: bfloat16 [8192, 1024], P(('dp', 'tensor')), may hold values from -6 to 6
- cotangent: bfloat16 [8192, 1024], P(('dp', 'tensor')), may hold values from -6 to 6
- attn_gain: float32 [1024], replicated, may hold values from 0.1 to 1.9
- q_gain: float32 [128], replicated, may hold values from 0.1 to 1.9
- k_gain: float32 [128], replicated, may hold values from 0.1 to 1.9
- mlp_gain: float32 [1024], replicated, may hold values from 0.1 to 1.9
- w_query: bfloat16 [1024, 2048], P(None, 'tensor'), may hold values from -0.1875 to 0.1875
- key_weight: bfloat16 [1024, 1024], P(None, 'tensor'), may hold values from -0.1875 to 0.1875
- value_weight: bfloat16 [1024, 1024], P(None, 'tensor'), may hold values from -0.1875 to 0.1875
- w_out: bfloat16 [2048, 1024], P('tensor'), may hold values from -0.75 to 0.75
- w_gate: bfloat16 [1024, 3072], P(None, 'tensor'), may hold values from -0.1875 to 0.1875
- w_up: bfloat16 [1024, 3072], P(None, 'tensor'), may hold values from -0.1875 to 0.1875
- w_down: bfloat16 [3072, 1024], P('tensor'), may hold values from -0.109375 to 0.109375
- lengths: int32 [8], P('dp'), may hold values from 512 to 1024, as said below
Outputs:
- layer_out: float32 [8192, 1024], P(('dp', 'tensor'))
- tokens_grad: float32 [8192, 1024], P(('dp', 'tensor'))
- attn_gain_grad: float32 [1024], replicated
- q_gain_grad: float32 [128], replicated
- k_gain_grad: float32 [128], replicated
- mlp_gain_grad: float32 [1024], replicated
- w_query_grad: float32 [1024, 2048], P(None, 'tensor')
- w_key_grad: float32 [1024, 1024], P(None, 'tensor')
- w_value_grad: float32 [1024, 1024], P(None, 'tensor')
- w_out_grad: float32 [2048, 1024], P('tensor')
- w_gate_grad: float32 [1024, 3072], P(None, 'tensor')
- w_up_grad: float32 [1024, 3072], P(None, 'tensor')
- w_down_grad: float32 [3072, 1024], P('tensor')
The draws below stay inside these ranges and needn't reach their ends.
Inputs may be any that keep to these rules, and one draw needn't show every extreme that they name: Sequence s fills rows 0 to lengths[s] - 1 of the 1024 rows of index s of dp; the other rows are padding. Some sequence has exactly 1024 tokens.
All inputs are finite; a program needn't handle non-finite values.
Results may differ from the reference program's by a relative error of at most 0.014.
Values may be sent and summed in bfloat16 or wider, within the bound.
No kernel may reach another device: no remote copies, remote signals or barrier semaphores. Data moves between devices by JAX's collectives and lax.ppermute only.
A program may use at most 128 MiB of HBM per device.

```python
import jax
import jax.numpy as jnp
from jax import lax

MODEL_WIDTH = 1024
QUERY_HEADS = 16
KEY_VALUE_HEADS = 8
HEAD_SIZE = 128
FF = 3072
CAP = 1024
QBLOCK = 512
LEAST = 512
TOKENS = 8192
N_DP = 8


def draw_lengths(key, part):
    first_key, second_key = jax.random.split(jax.random.fold_in(key, 17))
    drawn = jax.random.randint(first_key, (N_DP,), LEAST, CAP + 1)
    full_index = jax.random.randint(second_key, (), 0, N_DP)
    return jnp.where(jnp.arange(N_DP) == full_index, CAP, drawn).astype(jnp.int32)


def block_scale(stream_key, shape, pieces, smallest, high):
    def one(dim, parts):
        draws = jax.random.uniform(jax.random.fold_in(jax.random.fold_in(stream_key, 6), dim), (parts,), jnp.float32, smallest / len(pieces), high / len(pieces))
        return jnp.repeat(jnp.exp(draws), shape[dim] // parts).reshape((-1,) + (1,) * (len(shape) - dim - 1))

    level = one(*pieces[0])
    for cut in pieces[1:]:
        level = level * one(*cut)
    return level


def gaussian(rng, shape, deviation, reach, pieces=(), kind=jnp.bfloat16):
    factor_of = block_scale(rng, shape, pieces, -0.22, 0.18) if pieces else 1.0
    array = jax.random.normal(rng, shape, jnp.float32) * deviation * factor_of
    return jnp.minimum(jnp.maximum(array, -reach), reach).astype(kind)


def setup_inputs(seed: int = 0) -> dict:
    arg_keys = jax.random.split(jax.random.key(seed), 15)
    return {
        "tokens": gaussian(arg_keys[0], (TOKENS, MODEL_WIDTH), 1.0, 6.0, ((0, 32),)),
        "cotangent": gaussian(arg_keys[1], (TOKENS, MODEL_WIDTH), 1.0, 6.0, ((0, 32),)),
        "attn_gain": jnp.clip(1.0 + 0.18 * jax.random.normal(arg_keys[2], (MODEL_WIDTH,), jnp.float32), 0.1, 1.9),
        "q_gain": jnp.clip(1.0 + 0.18 * jax.random.normal(arg_keys[3], (HEAD_SIZE,), jnp.float32), 0.1, 1.9),
        "k_gain": jnp.clip(1.0 + 0.18 * jax.random.normal(arg_keys[4], (HEAD_SIZE,), jnp.float32), 0.1, 1.9),
        "mlp_gain": jnp.clip(1.0 + 0.18 * jax.random.normal(arg_keys[5], (MODEL_WIDTH,), jnp.float32), 0.1, 1.9),
        "w_query": gaussian(arg_keys[6], (MODEL_WIDTH, QUERY_HEADS * HEAD_SIZE), MODEL_WIDTH ** -0.5, 0.1875, ((1, 4),)),
        "key_weight": gaussian(arg_keys[7], (MODEL_WIDTH, KEY_VALUE_HEADS * HEAD_SIZE), MODEL_WIDTH ** -0.5, 0.1875, ((1, 4),)),
        "value_weight": gaussian(arg_keys[8], (MODEL_WIDTH, KEY_VALUE_HEADS * HEAD_SIZE), MODEL_WIDTH ** -0.5, 0.1875, ((1, 4),)),
        "w_out": gaussian(arg_keys[9], (QUERY_HEADS * HEAD_SIZE, MODEL_WIDTH), (max(1, QUERY_HEADS * HEAD_SIZE // 32)) ** -0.5, 0.75, ((0, 4),)),
        "w_gate": gaussian(arg_keys[10], (MODEL_WIDTH, FF), MODEL_WIDTH ** -0.5, 0.1875, ((1, 4),)),
        "w_up": gaussian(arg_keys[11], (MODEL_WIDTH, FF), MODEL_WIDTH ** -0.5, 0.1875, ((1, 4),)),
        "w_down": gaussian(arg_keys[12], (FF, MODEL_WIDTH), FF ** -0.5, 0.109375, ((0, 4),)),
        "lengths": draw_lengths(jax.random.fold_in(arg_keys[14], 71), 0),
    }


@jax.custom_vjp
def lower_setting(v):
    return lax.optimization_barrier(v.astype(jnp.bfloat16)).astype(jnp.float32)

@jax.custom_vjp
def lower_setting_backward(v):
    return v

def low_keep(v):
    return (lower_setting(v), None)

def low_pass(kept, grad):
    return (grad,)

def back_keep(v):
    return (v, None)

def back_low(kept, grad):
    return (lower_setting(grad),)
lower_setting.defvjp(low_keep, low_pass)
lower_setting_backward.defvjp(back_keep, back_low)
epsilon = 1e-06
rotary_base = 1000000.0
masked_score = -1e+30
highest_setting = lax.Precision.HIGHEST

def rms_norm(values, gain):
    return values * lax.rsqrt(lax.optimization_barrier(jnp.mean(values * values, axis=-1, keepdims=True)) + epsilon) * gain

def rotary(values):
    every_row = values.shape[0]
    half_width = HEAD_SIZE // 2
    frequency = rotary_base ** (-(jnp.arange(half_width, dtype=jnp.float32) * 2.0) / HEAD_SIZE)
    angles = jnp.arange(every_row, dtype=jnp.float32)[:, None] * frequency[None, :]
    cosine = jnp.concatenate([jnp.cos(angles), jnp.cos(angles)], axis=-1)[:, None, :]
    sine_table = jnp.concatenate([jnp.sin(angles), jnp.sin(angles)], axis=-1)[:, None, :]
    first = values[..., :half_width]
    second = values[..., half_width:]
    turned = jnp.concatenate([-second, first], axis=-1)
    return values * cosine + turned * sine_table

def sequence(seq_rows, length, attn_gain, q_gain, k_gain, mlp_gain, w_query, key_weight, value_weight, w_out, w_gate, w_up, w_down):
    every_row = seq_rows.shape[0]
    attention_normed_input = lower_setting(rms_norm(seq_rows, attn_gain))
    raw_q = lower_setting_backward(jnp.dot(attention_normed_input, w_query, precision=highest_setting)).reshape(every_row, QUERY_HEADS, HEAD_SIZE)
    unrotated_key = lower_setting_backward(jnp.dot(attention_normed_input, key_weight, precision=highest_setting)).reshape(every_row, KEY_VALUE_HEADS, HEAD_SIZE)
    value_rows = lower_setting(lower_setting_backward(jnp.dot(attention_normed_input, value_weight, precision=highest_setting))).reshape(every_row, KEY_VALUE_HEADS, HEAD_SIZE)
    query = lower_setting(rotary(rms_norm(raw_q, q_gain)))
    heads_of_key = lower_setting(rotary(rms_norm(unrotated_key, k_gain)))
    heads_of_key = jnp.repeat(heads_of_key, QUERY_HEADS // KEY_VALUE_HEADS, axis=1)
    value_rows = jnp.repeat(value_rows, QUERY_HEADS // KEY_VALUE_HEADS, axis=1)
    key_place = jnp.arange(every_row, dtype=jnp.int32)
    scaling = HEAD_SIZE ** (-0.5)

    def attend_block(block_index):
        block_start = block_index * QBLOCK
        block_q = lax.dynamic_slice_in_dim(query, block_start, QBLOCK, 0)
        scores = lower_setting_backward(scaling * jnp.einsum('qhd,khd->hqk', block_q, heads_of_key, precision=highest_setting))
        places = block_start + jnp.arange(QBLOCK, dtype=jnp.int32)
        allowed = (key_place[None, :] <= places[:, None]) & (key_place[None, :] < length)
        scores = jnp.where(allowed[None], scores, masked_score)
        row_max = lax.optimization_barrier(jnp.max(scores, axis=-1, keepdims=True))
        exponent = jnp.exp(scores - row_max)
        weights = lower_setting(exponent / lax.optimization_barrier(jnp.sum(exponent, axis=-1, keepdims=True)))
        return jnp.einsum('hqk,khd->qhd', weights, value_rows, precision=highest_setting)
    attended = lax.map(jax.checkpoint(attend_block), jnp.arange(every_row // QBLOCK, dtype=jnp.int32))
    attended = lower_setting(lower_setting_backward(attended.reshape(every_row, QUERY_HEADS * HEAD_SIZE)))
    mixed = seq_rows + lower_setting_backward(jnp.dot(attended, w_out, precision=highest_setting))
    normed_m = lower_setting(rms_norm(mixed, mlp_gain))
    gate_proj = lower_setting_backward(jnp.dot(normed_m, w_gate, precision=highest_setting))
    up_proj = lower_setting_backward(jnp.dot(normed_m, w_up, precision=highest_setting))
    activated = lower_setting(gate_proj / (1.0 + jnp.exp(-gate_proj)) * up_proj)
    result = mixed + lower_setting_backward(jnp.dot(activated, w_down, precision=highest_setting))
    live_rows = (key_place < length)[:, None]
    return jnp.where(live_rows, result, 0.0)

def reference(tokens, cotangent, attn_gain, q_gain, k_gain, mlp_gain, w_query, key_weight, value_weight, w_out, w_gate, w_up, w_down, lengths):
    floats = [a.astype(jnp.float32) for a in (tokens, attn_gain, q_gain, k_gain, mlp_gain, w_query, key_weight, value_weight, w_out, w_gate, w_up, w_down)]

    def forward(tokens_f, *params):
        sequences = tokens_f.reshape(N_DP, CAP, MODEL_WIDTH)

        def seq_step(state_carry, seq_item):
            seq_rows, length = seq_item
            return (state_carry, sequence(seq_rows, length, *params))
        _, outputs = lax.scan(seq_step, jnp.zeros((), jnp.float32), (sequences, lengths))
        return outputs.reshape(N_DP * CAP, MODEL_WIDTH)
    layer_out, pullback = jax.vjp(forward, *floats)
    gradients = pullback(cotangent.astype(jnp.float32))
    return (layer_out, gradients[0], gradients[1], gradients[2], gradients[3], gradients[4], gradients[5], gradients[6], gradients[7], gradients[8], gradients[9], gradients[10], gradients[11])
```

```python
import jax
import jax.numpy as jnp
from jax import lax
from jax.sharding import PartitionSpec as P

HEAD_SIZE = 128
QBLOCK = 512


epsilon = 1e-06
rotary_base = 1000000.0
masked_score = -1e30


def rms_norm(values, gain):
    return values * lax.rsqrt(jnp.mean(values * values, axis=-1, keepdims=True) + epsilon) * gain


def rotary(values):
    every_row = values.shape[0]
    half_width = HEAD_SIZE // 2
    frequency = rotary_base ** (-(jnp.arange(half_width, dtype=jnp.float32) * 2.0) / HEAD_SIZE)
    angles = jnp.arange(every_row, dtype=jnp.float32)[:, None] * frequency[None, :]
    cosine = jnp.concatenate([jnp.cos(angles), jnp.cos(angles)], axis=-1)[:, None, :]
    sine_table = jnp.concatenate([jnp.sin(angles), jnp.sin(angles)], axis=-1)[:, None, :]
    first = values[..., :half_width]
    second = values[..., half_width:]
    turned = jnp.concatenate([-second, first], axis=-1)
    return values * cosine + turned * sine_table


def shaped(raw_rows, gain, head_count):
    return rotary(rms_norm(raw_rows.reshape(raw_rows.shape[0], head_count, HEAD_SIZE), gain))


def swiglu(gate_proj, up_proj):
    return gate_proj / (1.0 + jnp.exp(-gate_proj)) * up_proj


def bit_of(axis, bit):
    return (lax.axis_index(axis) >> bit) & 1


def swap(values, axis, bit):
    size = lax.axis_size(axis)
    return lax.ppermute(values, axis, [(i, i ^ (1 << bit)) for i in range(size)])


def ordered_pair(mine, other, flag):
    is_first = flag == 0
    return jnp.concatenate(
        [jnp.where(is_first, mine, other), jnp.where(is_first, other, mine)], axis=0
    )


def halves(values, flag):
    rows = values.shape[0] // 2
    sent = lax.dynamic_slice_in_dim(values, (1 - flag) * rows, rows, 0)
    kept = lax.dynamic_slice_in_dim(values, flag * rows, rows, 0)
    return sent, kept


def spread(values):
    core = bit_of("tensor", 0)
    side = bit_of("tensor", 1)
    across = swap(values, "tensor", 1)
    near = swap(values, "tensor", 0)
    far = swap(across, "tensor", 0)
    return ordered_pair(
        ordered_pair(values, near, core), ordered_pair(across, far, core), side
    )


def settle(values):
    core = bit_of("tensor", 0)
    side = bit_of("tensor", 1)
    rows = values.shape[0] // 4
    parts = values.astype(jnp.bfloat16).reshape(2, 2, rows, values.shape[1])
    sent = lax.dynamic_slice_in_dim(parts, 1 - core, 1, 1)
    kept = lax.dynamic_slice_in_dim(parts, core, 1, 1)
    pair = (kept.astype(jnp.float32) + swap(sent, "tensor", 0).astype(jnp.float32))[:, 0]
    away = lax.dynamic_slice_in_dim(pair, 1 - side, 1, 0)[0].astype(jnp.bfloat16)
    home = lax.dynamic_slice_in_dim(pair, side, 1, 0)[0]
    return home + swap(away, "tensor", 1).astype(jnp.float32)


def bit_order(first):
    count = (lax.axis_size("dp") - 1).bit_length()
    return [(first + i) % count for i in range(count)]


def reduced_over_dp(values, first):
    order = bit_order(first)
    part = values.astype(jnp.bfloat16)
    for bit in order:
        sent, kept = halves(part, bit_of("dp", bit))
        part = (kept.astype(jnp.float32) + swap(sent, "dp", bit).astype(jnp.float32)).astype(
            jnp.bfloat16
        )
    for bit in reversed(order):
        part = ordered_pair(part, swap(part, "dp", bit), bit_of("dp", bit))
    return part.astype(jnp.float32)


def reduced_over_all(values):
    for axis in ("tensor", "dp"):
        for bit in range((lax.axis_size(axis) - 1).bit_length()):
            values = values + swap(values, axis, bit)
    return values


def unrolled(count, step, carry):
    for index in range(count):
        carry = step(index, carry)
    return carry


def body(
    tokens,
    cotangent,
    attn_gain,
    q_gain,
    k_gain,
    mlp_gain,
    w_query,
    key_weight,
    value_weight,
    w_out,
    w_gate,
    w_up,
    w_down,
    lengths,
):
    share_rows = tokens.shape[0]
    every_row = share_rows * lax.axis_size("tensor")
    q_heads = w_query.shape[1] // HEAD_SIZE
    kv_heads = key_weight.shape[1] // HEAD_SIZE
    head_group = q_heads // kv_heads
    length = lengths[0]
    first_row = lax.axis_index("tensor") * share_rows
    live_rows = (first_row + jnp.arange(share_rows, dtype=jnp.int32) < length)[:, None]
    resid = tokens.astype(jnp.float32)
    scaling = HEAD_SIZE ** (-0.5)
    whole_a = spread(rms_norm(resid, attn_gain).astype(jnp.bfloat16))
    raw_q = jnp.dot(whole_a, w_query, preferred_element_type=jnp.float32)
    unrotated_key = jnp.dot(whole_a, key_weight, preferred_element_type=jnp.float32)
    value_heads = (
        jnp.dot(whole_a, value_weight, preferred_element_type=jnp.float32)
        .astype(jnp.bfloat16)
        .reshape(every_row, kv_heads, HEAD_SIZE)
    )
    query_groups = (
        shaped(raw_q, q_gain, q_heads)
        .astype(jnp.bfloat16)
        .reshape(every_row, kv_heads, head_group, HEAD_SIZE)
    )
    heads_of_key = shaped(unrotated_key, k_gain, kv_heads).astype(jnp.bfloat16)
    key_place = jnp.arange(every_row, dtype=jnp.int32)

    def scores_of(block_start):
        block_q = lax.dynamic_slice_in_dim(query_groups, block_start, QBLOCK, 0)
        scores = (
            jnp.einsum("qgjd,kgd->gjqk", block_q, heads_of_key, preferred_element_type=jnp.float32)
            * scaling
        )
        places = block_start + jnp.arange(QBLOCK, dtype=jnp.int32)
        allowed = (key_place[None, :] <= places[:, None]) & (key_place[None, :] < length)
        return (block_q, jnp.where(allowed, scores, masked_score))

    def forward_block(block_index, state_carry):
        attended, lse_all = state_carry
        block_start = block_index * QBLOCK
        _, scores = scores_of(block_start)
        row_max = jnp.max(scores, axis=-1, keepdims=True)
        exponent = jnp.exp(scores - row_max)
        row_sum = jnp.sum(exponent, axis=-1, keepdims=True)
        weights = (exponent / row_sum).astype(jnp.bfloat16)
        block_out = jnp.einsum(
            "gjqk,kgd->qgjd", weights, value_heads, preferred_element_type=jnp.float32
        )
        block_out = block_out.reshape(QBLOCK, q_heads * HEAD_SIZE).astype(jnp.bfloat16)
        attended = lax.dynamic_update_slice_in_dim(attended, block_out, block_start, 0)
        lse_all = lax.dynamic_update_slice_in_dim(
            lse_all, (row_max + jnp.log(row_sum))[..., 0], block_start, 2
        )
        return (attended, lse_all)

    attended, lse_all = unrolled(
        every_row // QBLOCK,
        forward_block,
        (
            jnp.zeros((every_row, q_heads * HEAD_SIZE), jnp.bfloat16),
            jnp.zeros((kv_heads, head_group, every_row), jnp.float32),
        ),
    )
    mixed = resid + settle(jnp.dot(attended, w_out, preferred_element_type=jnp.float32))
    whole_m = spread(rms_norm(mixed, mlp_gain).astype(jnp.bfloat16))
    gate_proj = jnp.dot(whole_m, w_gate, preferred_element_type=jnp.float32)
    up_proj = jnp.dot(whole_m, w_up, preferred_element_type=jnp.float32)
    activated = swiglu(gate_proj, up_proj).astype(jnp.bfloat16)
    layer_out = jnp.where(
        live_rows,
        mixed + settle(jnp.dot(activated, w_down, preferred_element_type=jnp.float32)),
        0.0,
    )
    grad_out = jnp.where(live_rows, cotangent.astype(jnp.float32), 0.0)
    grad_ffn = spread(grad_out.astype(jnp.bfloat16))
    grad_w_down = jnp.einsum("rf,rd->fd", activated, grad_ffn, preferred_element_type=jnp.float32)
    grad_act = jnp.einsum("rd,fd->rf", grad_ffn, w_down, preferred_element_type=jnp.float32)
    _, swiglu_back = jax.vjp(swiglu, gate_proj, up_proj)
    grad_gate, grad_up = swiglu_back(grad_act)
    grad_gate = grad_gate.astype(jnp.bfloat16)
    grad_up = grad_up.astype(jnp.bfloat16)
    grad_w_gate = jnp.einsum("rd,rf->df", whole_m, grad_gate, preferred_element_type=jnp.float32)
    grad_w_up = jnp.einsum("rd,rf->df", whole_m, grad_up, preferred_element_type=jnp.float32)
    grad_normed_m = jnp.einsum(
        "rf,df->rd", grad_gate, w_gate, preferred_element_type=jnp.float32
    ) + jnp.einsum("rf,df->rd", grad_up, w_up, preferred_element_type=jnp.float32)
    _, mlp_norm_back = jax.vjp(rms_norm, mixed, mlp_gain)
    grad_mixed_norm, grad_mlp_gain = mlp_norm_back(settle(grad_normed_m))
    grad_mixed = grad_out + grad_mixed_norm
    grad_branch = spread(grad_mixed.astype(jnp.bfloat16))
    grad_w_out = jnp.einsum("rc,rd->cd", attended, grad_branch, preferred_element_type=jnp.float32)
    grad_groups = (
        jnp.einsum("rd,cd->rc", grad_branch, w_out, preferred_element_type=jnp.float32)
        .astype(jnp.bfloat16)
        .reshape(every_row, kv_heads, head_group, HEAD_SIZE)
    )

    def backward_block(block_index, state_carry):
        grad_query, grad_key, grad_value = state_carry
        block_start = block_index * QBLOCK
        block_q, scores = scores_of(block_start)
        block_lse = lax.dynamic_slice_in_dim(lse_all, block_start, QBLOCK, 2)
        probability = jnp.exp(scores - block_lse[..., None])
        block_grad = lax.dynamic_slice_in_dim(grad_groups, block_start, QBLOCK, 0)
        grad_probs = jnp.einsum(
            "qgjd,kgd->gjqk", block_grad, value_heads, preferred_element_type=jnp.float32
        )
        row_delta = jnp.sum(grad_probs * probability, axis=-1, keepdims=True)
        grad_scores = (probability * (grad_probs - row_delta)).astype(jnp.bfloat16)
        part_query = (
            jnp.einsum(
                "gjqk,kgd->qgjd", grad_scores, heads_of_key, preferred_element_type=jnp.float32
            )
            * scaling
        )
        grad_query = lax.dynamic_update_slice_in_dim(grad_query, part_query, block_start, 0)
        grad_key = (
            grad_key
            + jnp.einsum("gjqk,qgjd->kgd", grad_scores, block_q, preferred_element_type=jnp.float32)
            * scaling
        )
        grad_value = grad_value + jnp.einsum(
            "gjqk,qgjd->kgd",
            probability.astype(jnp.bfloat16),
            block_grad,
            preferred_element_type=jnp.float32,
        )
        return (grad_query, grad_key, grad_value)

    grad_query, grad_key, grad_value = unrolled(
        every_row // QBLOCK,
        backward_block,
        (
            jnp.zeros((every_row, kv_heads, head_group, HEAD_SIZE), jnp.float32),
            jnp.zeros((every_row, kv_heads, HEAD_SIZE), jnp.float32),
            jnp.zeros((every_row, kv_heads, HEAD_SIZE), jnp.float32),
        ),
    )
    _, query_back = jax.vjp(lambda raw_rows, gain: shaped(raw_rows, gain, q_heads), raw_q, q_gain)
    grad_raw_q, grad_q_gain = query_back(grad_query.reshape(every_row, q_heads, HEAD_SIZE))
    _, key_back = jax.vjp(
        lambda raw_rows, gain: shaped(raw_rows, gain, kv_heads), unrotated_key, k_gain
    )
    grad_raw_k, grad_k_gain = key_back(grad_key)
    grad_raw_q = grad_raw_q.astype(jnp.bfloat16)
    grad_raw_k = grad_raw_k.astype(jnp.bfloat16)
    grad_raw_v = grad_value.reshape(every_row, kv_heads * HEAD_SIZE).astype(jnp.bfloat16)
    grad_w_query = jnp.einsum("rd,rc->dc", whole_a, grad_raw_q, preferred_element_type=jnp.float32)
    grad_w_key = jnp.einsum("rd,rc->dc", whole_a, grad_raw_k, preferred_element_type=jnp.float32)
    grad_w_value = jnp.einsum("rd,rc->dc", whole_a, grad_raw_v, preferred_element_type=jnp.float32)
    grad_normed_a = jnp.einsum("rc,dc->rd", grad_raw_q, w_query, preferred_element_type=jnp.float32)
    grad_normed_a = grad_normed_a + jnp.einsum(
        "rc,dc->rd", grad_raw_k, key_weight, preferred_element_type=jnp.float32
    )
    grad_normed_a = grad_normed_a + jnp.einsum(
        "rc,dc->rd", grad_raw_v, value_weight, preferred_element_type=jnp.float32
    )
    _, attn_norm_back = jax.vjp(rms_norm, resid, attn_gain)
    grad_resid_norm, grad_attn_gain = attn_norm_back(settle(grad_normed_a))
    tokens_grad = grad_mixed + grad_resid_norm
    grad_w_down = reduced_over_dp(grad_w_down, 0)
    grad_w_gate = reduced_over_dp(grad_w_gate, 1)
    grad_w_up = reduced_over_dp(grad_w_up, 0)
    grad_w_out = reduced_over_dp(grad_w_out, 1)
    grad_w_query = reduced_over_dp(grad_w_query, 0)
    grad_w_key = reduced_over_dp(grad_w_key, 1)
    grad_w_value = reduced_over_dp(grad_w_value, 1)
    gains = reduced_over_all(
        jnp.concatenate([grad_attn_gain, grad_mlp_gain, grad_q_gain, grad_k_gain])
    )
    width = grad_attn_gain.shape[0]
    grad_attn_gain, grad_mlp_gain, grad_q_gain, grad_k_gain = jnp.split(
        gains, [width, 2 * width, 2 * width + HEAD_SIZE]
    )
    return (
        layer_out,
        tokens_grad,
        grad_attn_gain,
        grad_q_gain,
        grad_k_gain,
        grad_mlp_gain,
        grad_w_query,
        grad_w_key,
        grad_w_value,
        grad_w_out,
        grad_w_gate,
        grad_w_up,
        grad_w_down,
    )


def solution(mesh):
    return jax.shard_map(
        body,
        mesh=mesh,
        in_specs=(
            P(("dp", "tensor"), None),
            P(("dp", "tensor"), None),
            P(),
            P(),
            P(),
            P(),
            P(None, "tensor"),
            P(None, "tensor"),
            P(None, "tensor"),
            P("tensor", None),
            P(None, "tensor"),
            P(None, "tensor"),
            P("tensor", None),
            P("dp"),
        ),
        out_specs=(
            P(("dp", "tensor"), None),
            P(("dp", "tensor"), None),
            P(),
            P(),
            P(),
            P(),
            P(None, "tensor"),
            P(None, "tensor"),
            P(None, "tensor"),
            P("tensor", None),
            P(None, "tensor"),
            P(None, "tensor"),
            P("tensor", None),
        ),
        check_vma=False,
    )
```

```python
import jax
import jax.numpy as jnp
from jax import lax
from jax.experimental import pallas as pl
from jax.experimental.pallas import tpu as pltpu
from jax.sharding import PartitionSpec as P

HEAD_SIZE = 128
BLOCK_ROWS = 256
epsilon = 1e-06
rotary_base = 1000000.0
masked_score = -1e30


def rotary_tables(every_row):
    half_width = HEAD_SIZE // 2
    frequency = rotary_base ** (-(jnp.arange(half_width, dtype=jnp.float32) * 2.0) / HEAD_SIZE)
    angles = jnp.arange(every_row, dtype=jnp.float32)[:, None] * frequency[None, :]
    cosine = jnp.cos(angles)
    sine = jnp.sin(angles)
    return (
        jnp.concatenate([cosine, cosine], axis=-1),
        jnp.concatenate([-sine, sine], axis=-1),
    )


def turned(values):
    return pltpu.roll(values, HEAD_SIZE // 2, 1)


def shaped(raw, gain, cosine, sine):
    normed = raw * lax.rsqrt(jnp.mean(raw * raw, axis=-1, keepdims=True) + epsilon) * gain
    return normed * cosine + turned(normed) * sine


def shaped_back(grad, raw, gain, cosine, sine):
    factor = lax.rsqrt(jnp.mean(raw * raw, axis=-1, keepdims=True) + epsilon)
    unit = raw * factor
    grad_normed = grad * cosine - turned(grad) * sine
    grad_gain = jnp.sum(grad_normed * unit, axis=0, keepdims=True)
    scaled = grad_normed * gain
    grad_raw = factor * (scaled - unit * jnp.mean(scaled * unit, axis=-1, keepdims=True))
    return grad_raw, grad_gain


def dot(left, right, left_dim, right_dim):
    return lax.dot_general(
        left, right, (((left_dim,), (right_dim,)), ((), ())), preferred_element_type=jnp.float32
    )


def heads_kernel(
    rows_ref, wq_ref, wk_ref, wv_ref, q_gain_ref, k_gain_ref, cos_ref, sin_ref,
    raw_q_ref, raw_k_ref, query_ref, key_ref, value_ref,
):
    rows = rows_ref[...]
    cosine = cos_ref[...]
    sine = sin_ref[...]
    value_ref[...] = dot(rows, wv_ref[...], 1, 0).astype(jnp.bfloat16)
    for weight_ref, gain_ref, raw_ref, out_ref in (
        (wq_ref, q_gain_ref, raw_q_ref, query_ref),
        (wk_ref, k_gain_ref, raw_k_ref, key_ref),
    ):
        raw = dot(rows, weight_ref[...], 1, 0)
        raw_ref[...] = raw
        for head in range(raw.shape[1] // HEAD_SIZE):
            cut = slice(head * HEAD_SIZE, (head + 1) * HEAD_SIZE)
            out_ref[:, cut] = shaped(raw[:, cut], gain_ref[...], cosine, sine).astype(jnp.bfloat16)


def project_heads(rows, w_query, key_weight, value_weight, q_gain, k_gain, cosine, sine):
    every_row, width = rows.shape
    block = BLOCK_ROWS
    q_cols, k_cols = w_query.shape[1], key_weight.shape[1]

    def by_row(cols):
        return pl.BlockSpec((block, cols), lambda i: (i, 0))

    def whole(shape):
        return pl.BlockSpec(shape, lambda i: (0, 0))

    return pl.pallas_call(
        heads_kernel,
        grid=(every_row // block,),
        in_specs=[
            by_row(width),
            whole(w_query.shape),
            whole(key_weight.shape),
            whole(value_weight.shape),
            whole((1, HEAD_SIZE)),
            whole((1, HEAD_SIZE)),
            by_row(HEAD_SIZE),
            by_row(HEAD_SIZE),
        ],
        out_specs=[by_row(q_cols), by_row(k_cols), by_row(q_cols), by_row(k_cols), by_row(k_cols)],
        out_shape=[
            jax.ShapeDtypeStruct((every_row, q_cols), jnp.float32),
            jax.ShapeDtypeStruct((every_row, k_cols), jnp.float32),
            jax.ShapeDtypeStruct((every_row, q_cols), jnp.bfloat16),
            jax.ShapeDtypeStruct((every_row, k_cols), jnp.bfloat16),
            jax.ShapeDtypeStruct((every_row, k_cols), jnp.bfloat16),
        ],
        name="project_heads",
    )(
        rows, w_query, key_weight, value_weight,
        q_gain.reshape(1, HEAD_SIZE), k_gain.reshape(1, HEAD_SIZE), cosine, sine,
    )


def masked_exponents(query, key, first_row, length):
    scores = dot(query, key, 1, 1) * HEAD_SIZE ** (-0.5)
    row = first_row + lax.broadcasted_iota(jnp.int32, scores.shape, 0)
    place = lax.broadcasted_iota(jnp.int32, scores.shape, 1)
    allowed = (place <= row) & (place < length)
    scores = jnp.where(allowed, scores, masked_score)
    exponents = jnp.exp(scores - jnp.max(scores, axis=-1, keepdims=True))
    return exponents, 1.0 / jnp.sum(exponents, axis=-1, keepdims=True)


def attend_kernel(length_ref, query_ref, key_ref, value_ref, out_ref):
    length = length_ref[0]
    every_row = key_ref.shape[0]
    for first_row in range(0, every_row, BLOCK_ROWS):
        last = first_row + BLOCK_ROWS
        exponents, inverse = masked_exponents(
            query_ref[first_row:last, :], key_ref[:last, :], first_row, length
        )
        weights = (exponents * inverse).astype(jnp.bfloat16)
        out_ref[first_row:last, :] = dot(weights, value_ref[:last, :], 1, 0).astype(jnp.bfloat16)


def attend(lengths, query, key, value):
    every_row, q_cols = query.shape
    group = q_cols // key.shape[1]

    def head_spec(share):
        return pl.BlockSpec((every_row, HEAD_SIZE), lambda h, lengths: (0, h // share))

    return pl.pallas_call(
        attend_kernel,
        grid_spec=pltpu.PrefetchScalarGridSpec(
            num_scalar_prefetch=1,
            grid=(q_cols // HEAD_SIZE,),
            in_specs=[head_spec(1), head_spec(group), head_spec(group)],
            out_specs=head_spec(1),
        ),
        out_shape=jax.ShapeDtypeStruct((every_row, q_cols), jnp.bfloat16),
        name="attend",
    )(lengths, query, key, value)


def attend_back_kernel(
    length_ref, query_ref, key_ref, value_ref, grad_ref, raw_q_ref, raw_k_ref,
    q_gain_ref, k_gain_ref, cos_ref, sin_ref,
    out_ref, gain_q_ref, gain_k_ref,
    key_acc, value_acc,
):
    length = length_ref[0]
    every_row = key_ref.shape[0]
    group = query_ref.shape[1] // HEAD_SIZE
    scaling = HEAD_SIZE ** (-0.5)
    key_acc[...] = jnp.zeros_like(key_acc)
    value_acc[...] = jnp.zeros_like(value_acc)
    gain_q = jnp.zeros((1, HEAD_SIZE), jnp.float32)
    for head in range(group):
        cut = slice(head * HEAD_SIZE, (head + 1) * HEAD_SIZE)
        for first_row in range(0, every_row, BLOCK_ROWS):
            last = first_row + BLOCK_ROWS
            query = query_ref[first_row:last, cut]
            grad = grad_ref[first_row:last, cut]
            exponents, inverse = masked_exponents(query, key_ref[:last, :], first_row, length)
            probs = exponents * inverse
            grad_probs = dot(grad, value_ref[:last, :], 1, 1)
            delta = jnp.sum(grad_probs * probs, axis=-1, keepdims=True)
            grad_scores = (probs * (grad_probs - delta)).astype(jnp.bfloat16)
            grad_query = dot(grad_scores, key_ref[:last, :], 1, 0) * scaling
            key_acc[:last, :] += dot(grad_scores, query, 0, 0)
            value_acc[:last, :] += dot(probs.astype(jnp.bfloat16), grad, 0, 0)
            grad_raw, grad_gain = shaped_back(
                grad_query, raw_q_ref[first_row:last, cut], q_gain_ref[...],
                cos_ref[first_row:last, :], sin_ref[first_row:last, :],
            )
            out_ref[first_row:last, cut] = grad_raw.astype(jnp.bfloat16)
            gain_q += grad_gain
    gain_q_ref[...] = gain_q
    grad_raw, grad_gain = shaped_back(
        key_acc[...] * scaling, raw_k_ref[...], k_gain_ref[...], cos_ref[...], sin_ref[...]
    )
    key_col = group * HEAD_SIZE
    value_col = key_col + HEAD_SIZE
    out_ref[:, key_col:value_col] = grad_raw.astype(jnp.bfloat16)
    out_ref[:, value_col:] = value_acc[...].astype(jnp.bfloat16)
    gain_k_ref[...] = grad_gain


def attend_back(
    kv_head, lengths, query, key, value, grad, raw_q, raw_k, q_gain, k_gain, cosine, sine
):
    every_row, q_cols = query.shape
    group_cols = q_cols // key.shape[1] * HEAD_SIZE

    def cut(cols):
        return pl.BlockSpec((every_row, cols), lambda i, lengths: (0, kv_head))

    def whole(rows, cols):
        return pl.BlockSpec((rows, cols), lambda i, lengths: (0, 0))

    return pl.pallas_call(
        attend_back_kernel,
        grid_spec=pltpu.PrefetchScalarGridSpec(
            num_scalar_prefetch=1,
            grid=(1,),
            in_specs=[
                cut(group_cols), cut(HEAD_SIZE), cut(HEAD_SIZE), cut(group_cols),
                cut(group_cols), cut(HEAD_SIZE),
                whole(1, HEAD_SIZE), whole(1, HEAD_SIZE),
                whole(every_row, HEAD_SIZE), whole(every_row, HEAD_SIZE),
            ],
            out_specs=[
                whole(every_row, group_cols + 2 * HEAD_SIZE),
                whole(1, HEAD_SIZE), whole(1, HEAD_SIZE),
            ],
            scratch_shapes=[
                pltpu.VMEM((every_row, HEAD_SIZE), jnp.float32),
                pltpu.VMEM((every_row, HEAD_SIZE), jnp.float32),
            ],
        ),
        out_shape=[
            jax.ShapeDtypeStruct((every_row, group_cols + 2 * HEAD_SIZE), jnp.bfloat16),
            jax.ShapeDtypeStruct((1, HEAD_SIZE), jnp.float32),
            jax.ShapeDtypeStruct((1, HEAD_SIZE), jnp.float32),
        ],
        name="attend_back",
    )(
        lengths, query, key, value, grad, raw_q, raw_k,
        q_gain.reshape(1, HEAD_SIZE), k_gain.reshape(1, HEAD_SIZE), cosine, sine,
    )


def rms_norm(values, gain):
    return values * lax.rsqrt(jnp.mean(values * values, axis=-1, keepdims=True) + epsilon) * gain


def swiglu(gate_proj, up_proj):
    return gate_proj / (1.0 + jnp.exp(-gate_proj)) * up_proj


def matmul(left, right, left_dim, right_dim):
    return dot(left, right, left_dim, right_dim).astype(jnp.bfloat16)


def bit_of(axis, bit):
    return (lax.axis_index(axis) >> bit) & 1


def swap(values, axis, bit):
    size = lax.axis_size(axis)
    return lax.ppermute(values, axis, [(i, i ^ (1 << bit)) for i in range(size)])


def bits(axis):
    return list(range((lax.axis_size(axis) - 1).bit_length()))


def ordered_pair(mine, other, flag):
    is_first = flag == 0
    return jnp.concatenate(
        [jnp.where(is_first, mine, other), jnp.where(is_first, other, mine)], axis=0
    )


def halves(values, flag):
    rows = values.shape[0] // 2
    sent = lax.dynamic_slice_in_dim(values, (1 - flag) * rows, rows, 0)
    kept = lax.dynamic_slice_in_dim(values, flag * rows, rows, 0)
    return sent, kept


def after(values, done):
    return lax.optimization_barrier((values, done))[0]


class Flight:
    def __init__(self, received, arrival):
        self.received = received
        self.arrival = arrival


class Order:
    def __init__(self):
        self.clock = 0.0
        self.token = None
        self.free = {}
        self.sums = []

    def gate(self, values):
        return values if self.token is None else after(values, self.token)

    def step(self, us, function, *inputs):
        out = function(*self.gate(inputs))
        self.token = out
        self.clock += us
        return out

    def send(self, values, axis, bit):
        size = values.size * values.dtype.itemsize
        if axis == "tensor" and bit == 0:
            us = size / 400e3
        else:
            us = 2 * size / 87e3 * (2 if axis == "dp" and bit > 1 else 1)
        values = self.gate(values)
        received = swap(values, axis, bit)
        self.token = values
        self.clock += 1.6
        start = max(self.clock, self.free.get((axis, bit), 0.0))
        self.free[axis, bit] = start + us
        return Flight(received, start + us + 1.0)

    def fill(self, until):
        while True:
            waiting = [one for one in self.sums if one.flight is not None]
            if not waiting:
                break
            one = min(waiting, key=lambda one: one.flight.arrival)
            if one.flight.arrival > max(self.clock, until - 3.0):
                break
            self.clock = max(self.clock, one.flight.arrival)
            one.advance()

    def land(self, flight):
        self.fill(flight.arrival)
        self.clock = max(self.clock, flight.arrival)
        received = self.gate(flight.received)
        self.token = received
        return received

    def finish(self):
        self.fill(float("inf"))


class DpSum:
    def __init__(self, order, values, first):
        count = len(bits("dp"))
        self.order = order
        self.turns = [(first + i) % count for i in range(count)]
        self.stage = 0
        self.part = values
        order.sums.append(self)
        self.launch()

    def launch(self):
        count = len(self.turns)
        if self.stage < count:
            bit = self.turns[self.stage]
            sent, self.kept = halves(self.part, bit_of("dp", bit))
        elif self.stage < 2 * count:
            bit = self.turns[2 * count - 1 - self.stage]
            sent = self.part
        else:
            self.flight = None
            return
        self.order.clock += 1.0
        self.flight = self.order.send(sent, "dp", bit)

    def advance(self):
        count = len(self.turns)
        received = self.order.gate(self.flight.received)
        if self.stage < count:
            self.part = (self.kept.astype(jnp.float32) + received.astype(jnp.float32)).astype(
                jnp.bfloat16
            )
        else:
            bit = self.turns[2 * count - 1 - self.stage]
            self.part = ordered_pair(self.part, received, bit_of("dp", bit))
        self.order.token = self.part
        self.stage += 1
        self.launch()


class GainSum:
    def __init__(self, order, values):
        self.order = order
        self.part = values
        self.turns = [(axis, bit) for axis in ("tensor", "dp") for bit in bits(axis)]
        order.sums.append(self)
        self.launch()

    def launch(self):
        self.flight = self.order.send(self.part, *self.turns.pop(0)) if self.turns else None

    def advance(self):
        self.part = self.part + self.order.gate(self.flight.received)
        self.order.token = self.part
        self.launch()


class Spread:
    def __init__(self, order, values):
        self.order = order
        self.values = values
        self.across = order.send(values, "tensor", 1)
        self.near = order.send(values, "tensor", 0)

    def land(self):
        core = bit_of("tensor", 0)
        side = bit_of("tensor", 1)
        across = self.order.land(self.across)
        far = self.order.send(across, "tensor", 0)
        near = self.order.gate(self.near.received)
        return self.order.step(
            4.0,
            lambda values, near, across, far: ordered_pair(
                ordered_pair(values, near, core), ordered_pair(across, far, core), side
            ),
            self.values, near, across, far.received,
        )


class Settle:
    def __init__(self, order, values):
        self.order = order
        core = bit_of("tensor", 0)
        rows = values.shape[0] // 4
        parts = values.reshape(2, 2, rows, values.shape[1])
        sent = lax.dynamic_slice_in_dim(parts, 1 - core, 1, 1)
        self.kept = lax.dynamic_slice_in_dim(parts, core, 1, 1)
        self.flight = order.send(sent, "tensor", 0)

    def cross(self):
        side = bit_of("tensor", 1)
        received = self.order.land(self.flight)
        pair = (self.kept.astype(jnp.float32) + received.astype(jnp.float32))[:, 0]
        away = lax.dynamic_slice_in_dim(pair, 1 - side, 1, 0)[0].astype(jnp.bfloat16)
        self.home = lax.dynamic_slice_in_dim(pair, side, 1, 0)[0]
        self.order.clock += 2.0
        self.flight = self.order.send(away, "tensor", 1)

    def land(self):
        return self.home + self.order.land(self.flight).astype(jnp.float32)


def body(
    tokens,
    cotangent,
    attn_gain,
    q_gain,
    k_gain,
    mlp_gain,
    w_query,
    key_weight,
    value_weight,
    w_out,
    w_gate,
    w_up,
    w_down,
    lengths,
):
    share_rows = tokens.shape[0]
    every_row = share_rows * lax.axis_size("tensor")
    kv_heads = key_weight.shape[1] // HEAD_SIZE
    group_cols = w_query.shape[1] // kv_heads
    length = lengths[0]
    first_row = lax.axis_index("tensor") * share_rows
    live_rows = (first_row + jnp.arange(share_rows, dtype=jnp.int32) < length)[:, None]
    order = Order()

    resid = tokens.astype(jnp.float32)
    gather_a = Spread(order, rms_norm(resid, attn_gain).astype(jnp.bfloat16))
    cosine, sine = rotary_tables(every_row)
    grad_out = jnp.where(live_rows, cotangent.astype(jnp.float32), 0.0)
    head_weights = [
        jnp.concatenate(
            [
                w_query[:, head * group_cols : (head + 1) * group_cols],
                key_weight[:, head * HEAD_SIZE : (head + 1) * HEAD_SIZE],
                value_weight[:, head * HEAD_SIZE : (head + 1) * HEAD_SIZE],
            ],
            axis=1,
        )
        for head in range(kv_heads)
    ]
    whole_a = gather_a.land()
    gather_ffn = Spread(order, grad_out.astype(jnp.bfloat16))
    raw_q, raw_k, query, key, value = order.step(
        7.5,
        lambda rows: project_heads(
            rows, w_query, key_weight, value_weight, q_gain, k_gain, cosine, sine
        ),
        whole_a,
    )
    attended = order.step(
        11.0, lambda query, key, value: attend(lengths, query, key, value), query, key, value
    )
    branch_out = order.step(1.5, lambda rows: matmul(rows, w_out, 1, 0), attended)
    settle_mixed = Settle(order, branch_out)
    settle_mixed.cross()
    whole_ffn = gather_ffn.land()
    grad_act = order.step(2.0, lambda rows: matmul(rows, w_down, 1, 1), whole_ffn)
    mixed = resid + settle_mixed.land()

    order.clock += 2.0
    whole_m = Spread(order, rms_norm(mixed, mlp_gain).astype(jnp.bfloat16)).land()

    def hidden(rows, grad_act):
        gate_proj = dot(rows, w_gate, 1, 0)
        up_proj = dot(rows, w_up, 1, 0)
        activated, swiglu_back = jax.vjp(swiglu, gate_proj, up_proj)
        grad_gate, grad_up = swiglu_back(grad_act.astype(jnp.float32))
        return (
            activated.astype(jnp.bfloat16),
            grad_gate.astype(jnp.bfloat16),
            grad_up.astype(jnp.bfloat16),
        )

    activated, grad_gate, grad_up = order.step(7.5, hidden, whole_m, grad_act)
    grad_w_down = DpSum(
        order, order.step(2.0, lambda a, b: matmul(a, b, 0, 0), activated, whole_ffn), 0
    )
    grad_normed_m = order.step(
        4.0,
        lambda a, b: (dot(a, w_gate, 1, 1) + dot(b, w_up, 1, 1)).astype(jnp.bfloat16),
        grad_gate, grad_up,
    )
    settle_m = Settle(order, grad_normed_m)
    settle_m.cross()
    grad_w_gate = DpSum(
        order, order.step(2.0, lambda a, b: matmul(a, b, 0, 0), whole_m, grad_gate), 0
    )
    up_grad = order.step(2.0, lambda a, b: matmul(a, b, 0, 0), whole_m, grad_up)
    layer_branch = order.step(2.0, lambda rows: matmul(rows, w_down, 1, 0), activated)
    _, mlp_norm_back = jax.vjp(rms_norm, mixed, mlp_gain)
    grad_mixed_norm, grad_mlp_gain = mlp_norm_back(settle_m.land())
    grad_mixed = grad_out + grad_mixed_norm
    order.clock += 2.0
    gather_branch = Spread(order, grad_mixed.astype(jnp.bfloat16))
    grad_w_up = DpSum(order, up_grad, 1)
    settle_out = Settle(order, layer_branch)
    grad_branch = gather_branch.land()

    grad_attended = order.step(2.0, lambda rows: matmul(rows, w_out, 1, 1), grad_branch)
    settle_out.cross()
    order.fill(order.clock)
    grad_w_out = DpSum(
        order, order.step(2.0, lambda a, b: matmul(a, b, 0, 0), attended, grad_branch), 0
    )
    heads = []
    for head in range(kv_heads):
        out, head_q_gain, head_k_gain = order.step(
            12.5,
            lambda grad: attend_back(
                head, lengths, query, key, value, grad, raw_q, raw_k,
                q_gain, k_gain, cosine, sine,
            ),
            grad_attended,
        )
        grad_weights = DpSum(
            order, order.step(2.0, lambda a, b: matmul(a, b, 0, 0), whole_a, out), head % 2
        )
        heads.append((out, grad_weights, head_q_gain[0], head_k_gain[0]))
        order.fill(order.clock)
    grad_normed_a = order.step(
        3.0,
        lambda outs: sum(
            dot(out, weights, 1, 1) for out, weights in zip(outs, head_weights)
        ).astype(jnp.bfloat16),
        [one[0] for one in heads],
    )
    settle_a = Settle(order, grad_normed_a)
    settle_a.cross()
    layer_out = jnp.where(live_rows, mixed + settle_out.land(), 0.0)
    _, attn_norm_back = jax.vjp(rms_norm, resid, attn_gain)
    grad_resid_norm, grad_attn_gain = attn_norm_back(settle_a.land())
    tokens_grad = grad_mixed + grad_resid_norm
    gains = GainSum(
        order,
        jnp.concatenate(
            [
                grad_attn_gain,
                grad_mlp_gain,
                sum(one[2] for one in heads),
                sum(one[3] for one in heads),
            ]
        ),
    )
    order.finish()

    width = attn_gain.shape[0]
    grad_attn_gain, grad_mlp_gain, grad_q_gain, grad_k_gain = jnp.split(
        gains.part, [width, 2 * width, 2 * width + HEAD_SIZE]
    )
    by_head = [one[1].part.astype(jnp.float32) for one in heads]
    value_col = group_cols + HEAD_SIZE
    return (
        layer_out,
        tokens_grad,
        grad_attn_gain,
        grad_q_gain,
        grad_k_gain,
        grad_mlp_gain,
        jnp.concatenate([one[:, :group_cols] for one in by_head], axis=1),
        jnp.concatenate([one[:, group_cols:value_col] for one in by_head], axis=1),
        jnp.concatenate([one[:, value_col:] for one in by_head], axis=1),
        grad_w_out.part.astype(jnp.float32),
        grad_w_gate.part.astype(jnp.float32),
        grad_w_up.part.astype(jnp.float32),
        grad_w_down.part.astype(jnp.float32),
    )


def solution(mesh):
    return jax.shard_map(
        body,
        mesh=mesh,
        in_specs=(
            P(("dp", "tensor"), None),
            P(("dp", "tensor"), None),
            P(),
            P(),
            P(),
            P(),
            P(None, "tensor"),
            P(None, "tensor"),
            P(None, "tensor"),
            P("tensor", None),
            P(None, "tensor"),
            P(None, "tensor"),
            P("tensor", None),
            P("dp"),
        ),
        out_specs=(
            P(("dp", "tensor"), None),
            P(("dp", "tensor"), None),
            P(),
            P(),
            P(),
            P(),
            P(None, "tensor"),
            P(None, "tensor"),
            P(None, "tensor"),
            P("tensor", None),
            P(None, "tensor"),
            P(None, "tensor"),
            P("tensor", None),
        ),
        check_vma=False,
    )
```

```python
import jax
import jax.numpy as jnp
from jax import lax
from jax.experimental import pallas as pl
from jax.experimental.pallas import tpu as pltpu
from jax.sharding import PartitionSpec as P

HEAD_SIZE = 128
BLOCK_ROWS = 256
epsilon = 1e-06
rotary_base = 1000000.0


def rotary_tables(every_row):
    half_width = HEAD_SIZE // 2
    frequency = rotary_base ** (-(jnp.arange(half_width, dtype=jnp.float32) * 2.0) / HEAD_SIZE)
    angles = jnp.arange(every_row, dtype=jnp.float32)[:, None] * frequency[None, :]
    cosine = jnp.cos(angles)
    sine = jnp.sin(angles)
    return (
        jnp.concatenate([cosine, cosine], axis=-1),
        jnp.concatenate([-sine, sine], axis=-1),
    )


def turned(values):
    return pltpu.roll(values, HEAD_SIZE // 2, 1)


def shaped(raw, gain, cosine, sine):
    normed = raw * lax.rsqrt(jnp.mean(raw * raw, axis=-1, keepdims=True) + epsilon) * gain
    return normed * cosine + turned(normed) * sine


def shaped_back(grad, raw, gain, cosine, sine):
    factor = lax.rsqrt(jnp.mean(raw * raw, axis=-1, keepdims=True) + epsilon)
    unit = raw * factor
    grad_normed = grad * cosine - turned(grad) * sine
    grad_gain = jnp.sum(grad_normed * unit, axis=0, keepdims=True)
    scaled = grad_normed * gain
    grad_raw = factor * (scaled - unit * jnp.mean(scaled * unit, axis=-1, keepdims=True))
    return grad_raw, grad_gain


def dot(left, right, left_dim, right_dim):
    return lax.dot_general(
        left, right, (((left_dim,), (right_dim,)), ((), ())), preferred_element_type=jnp.float32
    )


def heads_kernel(
    place_ref, mine_ref, near_ref, across_ref, far_ref, wq_ref, wk_ref, wv_ref, q_gain_ref, k_gain_ref, cos_ref, sin_ref,
    rows_ref, raw_q_ref, raw_k_ref, query_ref, key_ref, value_ref,
):
    for k, piece_ref in enumerate((mine_ref, near_ref, across_ref, far_ref)):

        @pl.when(pl.program_id(0) == k)
        def _():
            rows_ref[...] = piece_ref[...]

    rows = rows_ref[...]
    cosine = cos_ref[...]
    sine = sin_ref[...]
    value_ref[...] = dot(rows, wv_ref[...], 1, 0).astype(jnp.bfloat16)
    for weight_ref, gain_ref, raw_ref, out_ref in (
        (wq_ref, q_gain_ref, raw_q_ref, query_ref),
        (wk_ref, k_gain_ref, raw_k_ref, key_ref),
    ):
        raw = dot(rows, weight_ref[...], 1, 0)
        raw_ref[...] = raw
        for head in range(raw.shape[1] // HEAD_SIZE):
            cut = slice(head * HEAD_SIZE, (head + 1) * HEAD_SIZE)
            out_ref[:, cut] = shaped(raw[:, cut], gain_ref[...], cosine, sine).astype(jnp.bfloat16)


def project_heads(places, pieces, w_query, key_weight, value_weight, q_gain, k_gain, cosine, sine):
    block, width = pieces[0].shape
    every_row = block * len(pieces)
    q_cols, k_cols = w_query.shape[1], key_weight.shape[1]

    def by_row(cols):
        return pl.BlockSpec((block, cols), lambda i, places: (places[i], 0))

    def whole(shape):
        return pl.BlockSpec(shape, lambda i, places: (0, 0))

    outs = [
        (width, jnp.bfloat16), (q_cols, jnp.float32), (k_cols, jnp.float32),
        (q_cols, jnp.bfloat16), (k_cols, jnp.bfloat16), (k_cols, jnp.bfloat16),
    ]
    return pl.pallas_call(
        heads_kernel,
        grid_spec=pltpu.PrefetchScalarGridSpec(
            num_scalar_prefetch=1,
            grid=(len(pieces),),
            in_specs=[whole(one.shape) for one in pieces]
            + [
                whole(w_query.shape),
                whole(key_weight.shape),
                whole(value_weight.shape),
                whole((1, HEAD_SIZE)),
                whole((1, HEAD_SIZE)),
                by_row(HEAD_SIZE),
                by_row(HEAD_SIZE),
            ],
            out_specs=[by_row(cols) for cols, _ in outs],
        ),
        out_shape=[jax.ShapeDtypeStruct((every_row, cols), kind) for cols, kind in outs],
        name="project_heads",
    )(
        places, *pieces, w_query, key_weight, value_weight,
        q_gain.reshape(1, HEAD_SIZE), k_gain.reshape(1, HEAD_SIZE), cosine, sine,
    )


def live_lanes(length, every_row):
    row = lax.broadcasted_iota(jnp.int32, (every_row, HEAD_SIZE), 0)
    return jnp.where(row < length, 1.0, 0.0)


def exponents(query, key, diagonal):
    raised = jnp.exp2(dot(query, key, 1, 1) * (HEAD_SIZE ** (-0.5) * 1.4426950408889634))
    if diagonal:
        row = lax.broadcasted_iota(jnp.int32, raised.shape, 0)
        place = lax.broadcasted_iota(jnp.int32, raised.shape, 1)
        raised = jnp.where(place <= row, raised, 0.0)
    return raised


def spans(first_row):
    whole = [(slice(0, first_row), False)] if first_row else []
    return whole + [(slice(first_row, first_row + BLOCK_ROWS), True)]


def attend_kernel(length_ref, query_ref, key_ref, value_ref, out_ref):
    every_row = key_ref.shape[0]
    live = live_lanes(length_ref[0], every_row)
    values = jnp.concatenate(
        [(value_ref[...].astype(jnp.float32) * live).astype(jnp.bfloat16), live.astype(jnp.bfloat16)],
        axis=1,
    )
    for first_row in range(0, every_row, BLOCK_ROWS):
        rows = slice(first_row, first_row + BLOCK_ROWS)
        total = 0.0
        for span, diagonal in spans(first_row):
            raised = exponents(query_ref[rows, :], key_ref[span, :], diagonal)
            total = total + dot(raised.astype(jnp.bfloat16), values[span], 1, 0)
        out_ref[rows, :] = (total[:, :HEAD_SIZE] / total[:, HEAD_SIZE:]).astype(jnp.bfloat16)


def attend(lengths, query, key, value):
    every_row, q_cols = query.shape
    group = q_cols // key.shape[1]

    def head_spec(share):
        return pl.BlockSpec((every_row, HEAD_SIZE), lambda h, lengths: (0, h // share))

    return pl.pallas_call(
        attend_kernel,
        grid_spec=pltpu.PrefetchScalarGridSpec(
            num_scalar_prefetch=1,
            grid=(q_cols // HEAD_SIZE,),
            in_specs=[head_spec(1), head_spec(group), head_spec(group)],
            out_specs=head_spec(1),
        ),
        out_shape=jax.ShapeDtypeStruct((every_row, q_cols), jnp.bfloat16),
        name="attend",
    )(lengths, query, key, value)


def attend_back_kernel(
    length_ref, query_ref, key_ref, value_ref, attended_ref, grad_ref, raw_q_ref, raw_k_ref,
    q_gain_ref, k_gain_ref, cos_ref, sin_ref,
    out_ref, gain_q_ref, gain_k_ref,
    key_acc, value_acc,
):
    every_row = key_ref.shape[0]
    group = query_ref.shape[1] // HEAD_SIZE
    scaling = HEAD_SIZE ** (-0.5)
    live = live_lanes(length_ref[0], every_row)
    ones = live.astype(jnp.bfloat16)
    keys = (key_ref[...].astype(jnp.float32) * live).astype(jnp.bfloat16)
    key_acc[...] = jnp.zeros_like(key_acc)
    value_acc[...] = jnp.zeros_like(value_acc)
    gain_q = jnp.zeros((1, HEAD_SIZE), jnp.float32)
    for head in range(group):
        cut = slice(head * HEAD_SIZE, (head + 1) * HEAD_SIZE)
        for first_row in range(0, every_row, BLOCK_ROWS):
            rows = slice(first_row, first_row + BLOCK_ROWS)
            query = query_ref[rows, cut]
            grad = grad_ref[rows, cut]
            grad_wide = grad.astype(jnp.float32)
            delta = jnp.sum(
                grad_wide * attended_ref[rows, cut].astype(jnp.float32), axis=-1, keepdims=True
            )
            sums = 0.0
            grad_query = 0.0
            parts = []
            for span, diagonal in spans(first_row):
                raised = exponents(query, key_ref[span, :], diagonal)
                grad_scores = raised * (dot(grad, value_ref[span, :], 1, 1) - delta)
                raised = raised.astype(jnp.bfloat16)
                grad_scores = grad_scores.astype(jnp.bfloat16)
                sums = sums + dot(raised, ones[span], 1, 0)
                grad_query = grad_query + dot(grad_scores, keys[span], 1, 0)
                parts.append((span, raised, grad_scores))
            inverse = 1.0 / sums
            query_share = (query.astype(jnp.float32) * inverse).astype(jnp.bfloat16)
            grad_share = (grad_wide * inverse).astype(jnp.bfloat16)
            for span, raised, grad_scores in parts:
                key_acc[span, :] += dot(grad_scores, query_share, 0, 0)
                value_acc[span, :] += dot(raised, grad_share, 0, 0)
            grad_raw, grad_gain = shaped_back(
                grad_query * (inverse * scaling), raw_q_ref[rows, cut], q_gain_ref[...],
                cos_ref[rows, :], sin_ref[rows, :],
            )
            out_ref[rows, cut] = grad_raw.astype(jnp.bfloat16)
            gain_q += grad_gain
    gain_q_ref[...] = gain_q
    grad_raw, grad_gain = shaped_back(
        key_acc[...] * (live * scaling), raw_k_ref[...], k_gain_ref[...], cos_ref[...], sin_ref[...]
    )
    key_col = group * HEAD_SIZE
    value_col = key_col + HEAD_SIZE
    out_ref[:, key_col:value_col] = grad_raw.astype(jnp.bfloat16)
    out_ref[:, value_col:] = (value_acc[...] * live).astype(jnp.bfloat16)
    gain_k_ref[...] = grad_gain


def attend_back(
    kv_head, lengths, query, key, value, attended, grad, raw_q, raw_k, q_gain, k_gain, cosine, sine
):
    every_row, q_cols = query.shape
    group_cols = q_cols // key.shape[1] * HEAD_SIZE

    def cut(cols):
        return pl.BlockSpec((every_row, cols), lambda i, lengths: (0, kv_head))

    def whole(rows, cols):
        return pl.BlockSpec((rows, cols), lambda i, lengths: (0, 0))

    return pl.pallas_call(
        attend_back_kernel,
        grid_spec=pltpu.PrefetchScalarGridSpec(
            num_scalar_prefetch=1,
            grid=(1,),
            in_specs=[
                cut(group_cols), cut(HEAD_SIZE), cut(HEAD_SIZE), cut(group_cols),
                cut(group_cols), cut(group_cols), cut(HEAD_SIZE),
                whole(1, HEAD_SIZE), whole(1, HEAD_SIZE),
                whole(every_row, HEAD_SIZE), whole(every_row, HEAD_SIZE),
            ],
            out_specs=[
                whole(every_row, group_cols + 2 * HEAD_SIZE),
                whole(1, HEAD_SIZE), whole(1, HEAD_SIZE),
            ],
            scratch_shapes=[
                pltpu.VMEM((every_row, HEAD_SIZE), jnp.float32),
                pltpu.VMEM((every_row, HEAD_SIZE), jnp.float32),
            ],
        ),
        out_shape=[
            jax.ShapeDtypeStruct((every_row, group_cols + 2 * HEAD_SIZE), jnp.bfloat16),
            jax.ShapeDtypeStruct((1, HEAD_SIZE), jnp.float32),
            jax.ShapeDtypeStruct((1, HEAD_SIZE), jnp.float32),
        ],
        name="attend_back",
    )(
        lengths, query, key, value, attended, grad, raw_q, raw_k,
        q_gain.reshape(1, HEAD_SIZE), k_gain.reshape(1, HEAD_SIZE), cosine, sine,
    )


def rows_at(block, rows):
    return pl.ds(pl.multiple_of(block * rows, rows), rows)


def join_kernel(place_ref, *refs):
    for k, piece_ref in enumerate(refs[:-1]):
        rows = piece_ref.shape[0]
        refs[-1][rows_at(place_ref[k], rows), :] = piece_ref[...].astype(refs[-1].dtype)


def in_vmem(count):
    return [pl.BlockSpec(memory_space=pltpu.VMEM)] * count


def join(places, pieces, dtype=jnp.bfloat16):
    rows, width = pieces[0].shape
    count = len(pieces)
    if rows % 16:
        return jnp.stack(pieces)[jnp.argsort(places)].reshape(count * rows, width).astype(dtype)
    return pl.pallas_call(
        join_kernel,
        in_specs=[pl.BlockSpec(memory_space=pltpu.SMEM)] + in_vmem(count),
        out_specs=in_vmem(1)[0],
        out_shape=jax.ShapeDtypeStruct((count * rows, width), dtype),
        name="join",
    )(places, *pieces)


def rms_norm(values, gain):
    return values * lax.rsqrt(jnp.mean(values * values, axis=-1, keepdims=True) + epsilon) * gain


def swiglu(gate_proj, up_proj):
    return gate_proj / (1.0 + jnp.exp(-gate_proj)) * up_proj


def matmul(left, right, left_dim, right_dim):
    return dot(left, right, left_dim, right_dim).astype(jnp.bfloat16)


def bit_of(axis, bit):
    return (lax.axis_index(axis) >> bit) & 1


def swap(values, axis, bit):
    size = lax.axis_size(axis)
    return lax.ppermute(values, axis, [(i, i ^ (1 << bit)) for i in range(size)])


def bits(axis):
    return list(range((lax.axis_size(axis) - 1).bit_length()))


def ordered_pair(mine, other, flag):
    is_first = flag == 0
    return jnp.concatenate(
        [jnp.where(is_first, mine, other), jnp.where(is_first, other, mine)], axis=0
    )


def halves(values, flag):
    rows = values.shape[0] // 2
    sent = lax.dynamic_slice_in_dim(values, (1 - flag) * rows, rows, 0)
    kept = lax.dynamic_slice_in_dim(values, flag * rows, rows, 0)
    return sent, kept


def after(values, done):
    return lax.optimization_barrier((values, done))[0]


class Flight:
    def __init__(self, received, arrival):
        self.received = received
        self.arrival = arrival


class Order:
    def __init__(self):
        self.clock = 0.0
        self.token = None
        self.free = {}
        self.sums = []

    def gate(self, values):
        return values if self.token is None else after(values, self.token)

    def step(self, us, function, *inputs):
        out = function(*self.gate(inputs))
        self.token = out
        self.clock += us
        return out

    def send(self, values, axis, bit):
        size = values.size * values.dtype.itemsize
        if axis == "tensor" and bit == 0:
            us = size / 400e3
        else:
            us = 2 * size / 87e3 * (2 if axis == "dp" and bit > 1 else 1)
        values = self.gate(values)
        received = swap(values, axis, bit)
        self.token = values
        self.clock += 1.6
        start = max(self.clock, self.free.get((axis, bit), 0.0))
        self.free[axis, bit] = start + us
        return Flight(received, start + us + 1.0)

    def fill(self, until):
        while True:
            waiting = [one for one in self.sums if one.flight is not None]
            if not waiting:
                break
            one = min(waiting, key=lambda one: one.flight.arrival)
            if one.flight.arrival > max(self.clock, until - 3.0):
                break
            self.clock = max(self.clock, one.flight.arrival)
            one.advance()

    def land(self, flight):
        self.fill(flight.arrival)
        self.clock = max(self.clock, flight.arrival)
        received = self.gate(flight.received)
        self.token = received
        return received

    def finish(self):
        self.fill(float("inf"))


class DpSum:
    def __init__(self, order, values, first):
        turns = bits("dp")
        self.order = order
        self.turns = turns[first:] + turns[:first]
        self.stage = 0
        self.rows = values.shape[0]
        self.terms = [(values, 0)]
        order.sums.append(self)
        self.launch()

    def total(self, start):
        parts = [
            lax.dynamic_slice_in_dim(values, first + start, self.rows, 0).astype(jnp.float32)
            for values, first in self.terms
        ]
        return sum(parts[1:], parts[0]).astype(jnp.bfloat16)

    def launch(self):
        count = len(self.turns)
        if self.stage < count:
            bit = self.turns[self.stage]
            self.rows //= 2
            flag = bit_of("dp", bit)
            sent = self.total((1 - flag) * self.rows)
            self.terms = [(values, first + flag * self.rows) for values, first in self.terms]
        else:
            bit = self.turns[2 * count - 1 - self.stage]
            if self.stage == count:
                self.part = self.total(0)
            sent = self.part
        self.order.clock += 0.8
        self.flight = self.order.send(sent, "dp", bit)

    def advance(self):
        count = len(self.turns)
        received = self.order.gate(self.flight.received)
        self.order.token = received
        self.stage += 1
        if self.stage <= count:
            self.terms = self.terms + [(received, 0)]
        else:
            self.flag = bit_of("dp", self.turns[2 * count - self.stage])
            self.last = (self.part, received)
            self.part = ordered_pair(*self.last, self.flag)
            self.order.token = self.part
            self.order.clock += 1.0
            if self.stage == 2 * count:
                self.flight = None
                return
        self.launch()


class GainSum:
    def __init__(self, order, values):
        self.order = order
        self.part = values
        self.turns = [(axis, bit) for axis in ("tensor", "dp") for bit in bits(axis)]
        order.sums.append(self)
        self.launch()

    def launch(self):
        self.flight = self.order.send(self.part, *self.turns.pop(0)) if self.turns else None
        if self.flight is not None:
            self.flight.arrival += 12.0

    def advance(self):
        self.part = self.part + self.order.gate(self.flight.received)
        self.order.token = self.part
        self.launch()


class Spread:
    def __init__(self, order, values):
        self.order = order
        self.values = values
        self.across = order.send(values, "tensor", 1)
        self.near = order.send(values, "tensor", 0)

    def pieces(self):
        across = self.order.land(self.across)
        far = self.order.send(across, "tensor", 0)
        near = self.order.gate(self.near.received)
        return [self.values, near, across, far.received]

    def land(self, places):
        return self.order.step(2.0, lambda *pieces: join(places, pieces), *self.pieces())


class Settle:
    def __init__(self, order, values):
        self.order = order
        core = bit_of("tensor", 0)
        rows = values.shape[0] // 4
        parts = values.reshape(2, 2, rows, values.shape[1])
        sent = lax.dynamic_slice_in_dim(parts, 1 - core, 1, 1)
        self.kept = lax.dynamic_slice_in_dim(parts, core, 1, 1)
        self.flight = order.send(sent, "tensor", 0)

    def cross(self):
        side = bit_of("tensor", 1)
        received = self.order.land(self.flight)
        pair = (self.kept.astype(jnp.float32) + received.astype(jnp.float32))[:, 0]
        away = lax.dynamic_slice_in_dim(pair, 1 - side, 1, 0)[0].astype(jnp.bfloat16)
        self.home = lax.dynamic_slice_in_dim(pair, side, 1, 0)[0]
        self.order.clock += 2.0
        self.flight = self.order.send(away, "tensor", 1)

    def land(self):
        return self.home + self.order.land(self.flight).astype(jnp.float32)


class SettlePieces:
    def __init__(self, order, us, function, near_far, mine_across):
        self.order = order
        self.flight = order.send(order.step(us, function, near_far), "tensor", 0)
        self.kept = order.step(us, function, mine_across)

    def cross(self):
        self.near = self.order.land(self.flight)
        rows = self.near.shape[0] // 2
        self.order.clock += 1.0
        away = self.kept[rows:].astype(jnp.float32) + self.near[rows:].astype(jnp.float32)
        self.flight = self.order.send(away.astype(jnp.bfloat16), "tensor", 1)

    def land(self):
        received = self.order.land(self.flight).astype(jnp.float32)
        kept, near = after((self.kept, self.near), received)
        rows = near.shape[0] // 2
        return kept[:rows].astype(jnp.float32) + near[:rows].astype(jnp.float32) + received


def body(
    tokens,
    cotangent,
    attn_gain,
    q_gain,
    k_gain,
    mlp_gain,
    w_query,
    key_weight,
    value_weight,
    w_out,
    w_gate,
    w_up,
    w_down,
    lengths,
):
    share_rows = tokens.shape[0]
    every_row = share_rows * lax.axis_size("tensor")
    kv_heads = key_weight.shape[1] // HEAD_SIZE
    group_cols = w_query.shape[1] // kv_heads
    length = lengths[0]
    first_row = lax.axis_index("tensor") * share_rows
    live_rows = (first_row + jnp.arange(share_rows, dtype=jnp.int32) < length)[:, None]
    order = Order()

    core = bit_of("tensor", 0)
    side = bit_of("tensor", 1)
    turn = jnp.arange(4, dtype=jnp.int32)
    places = (side ^ (turn >> 1)) * 2 + (core ^ (turn & 1))

    resid = tokens.astype(jnp.float32)
    gather_a = Spread(order, rms_norm(resid, attn_gain).astype(jnp.bfloat16))
    cosine, sine = rotary_tables(every_row)
    grad_out = jnp.where(live_rows, cotangent.astype(jnp.float32), 0.0)
    head_weights = [
        jnp.concatenate(
            [
                w_query[:, head * group_cols : (head + 1) * group_cols],
                key_weight[:, head * HEAD_SIZE : (head + 1) * HEAD_SIZE],
                value_weight[:, head * HEAD_SIZE : (head + 1) * HEAD_SIZE],
            ],
            axis=1,
        )
        for head in range(kv_heads)
    ]
    pieces_a = gather_a.pieces()
    gather_ffn = Spread(order, grad_out.astype(jnp.bfloat16))
    whole_a, raw_q, raw_k, query, key, value = order.step(
        7.5,
        lambda *pieces: project_heads(
            places, pieces, w_query, key_weight, value_weight, q_gain, k_gain, cosine, sine
        ),
        *pieces_a,
    )
    attended = order.step(
        11.0, lambda query, key, value: attend(lengths, query, key, value), query, key, value
    )
    whole_ffn = jnp.concatenate(gather_ffn.pieces(), axis=0)
    branch_out = order.step(1.5, lambda rows: matmul(rows, w_out, 1, 0), attended)
    settle_mixed = Settle(order, branch_out)
    settle_mixed.cross()
    grad_act = order.step(2.0, lambda rows: matmul(rows, w_down, 1, 1), whole_ffn)
    mixed = resid + settle_mixed.land()

    order.clock += 2.0
    gather_m = Spread(order, rms_norm(mixed, mlp_gain).astype(jnp.bfloat16))

    def hidden(rows, grad_act):
        gate_proj = dot(rows, w_gate, 1, 0)
        up_proj = dot(rows, w_up, 1, 0)
        activated, swiglu_back = jax.vjp(swiglu, gate_proj, up_proj)
        grad_gate, grad_up = swiglu_back(grad_act.astype(jnp.float32))
        return (
            activated.astype(jnp.bfloat16),
            grad_gate.astype(jnp.bfloat16),
            grad_up.astype(jnp.bfloat16),
        )

    near_m = jnp.concatenate([gather_m.values, gather_m.near.received], axis=0)
    half = near_m.shape[0]
    near_hidden = order.step(4.0, hidden, near_m, grad_act[:half])
    far_m = jnp.concatenate(gather_m.pieces()[2:], axis=0)
    far_hidden = order.step(4.0, hidden, far_m, grad_act[half:])
    whole_m = jnp.concatenate([near_m, far_m], axis=0)
    activated, grad_gate, grad_up = [
        jnp.concatenate(both, axis=0) for both in zip(near_hidden, far_hidden)
    ]
    quarter = half // 2
    near_far = [
        jnp.concatenate([near[quarter:], far[quarter:]], axis=0)
        for near, far in zip(near_hidden, far_hidden)
    ]
    mine_across = [
        jnp.concatenate([near[:quarter], far[:quarter]], axis=0)
        for near, far in zip(near_hidden, far_hidden)
    ]
    grad_w_down = DpSum(
        order, order.step(2.0, lambda a, b: matmul(a, b, 0, 0), activated, whole_ffn), 0
    )
    grad_normed_m = order.step(
        4.0,
        lambda a, b: (dot(a, w_gate, 1, 1) + dot(b, w_up, 1, 1)).astype(jnp.bfloat16),
        grad_gate, grad_up,
    )
    settle_m = SettlePieces(
        order, 2.0,
        lambda grads: (dot(grads[1], w_gate, 1, 1) + dot(grads[2], w_up, 1, 1)).astype(jnp.bfloat16),
        near_far, mine_across,
    )
    settle_m.cross()
    grad_w_gate = DpSum(
        order, order.step(2.0, lambda a, b: matmul(a, b, 0, 0), whole_m, grad_gate), 0
    )
    up_grad = order.step(2.0, lambda a, b: matmul(a, b, 0, 0), whole_m, grad_up)
    _, mlp_norm_back = jax.vjp(rms_norm, mixed, mlp_gain)
    grad_mixed_norm, grad_mlp_gain = mlp_norm_back(settle_m.land())
    grad_mixed = grad_out + grad_mixed_norm
    order.clock += 2.0
    gather_branch = Spread(order, grad_mixed.astype(jnp.bfloat16))
    grad_w_up = DpSum(order, up_grad, 1)
    settle_out = SettlePieces(
        order, 1.5, lambda rows: matmul(rows[0], w_down, 1, 0), near_far, mine_across
    )
    grad_branch = gather_branch.land(places)

    grad_attended = order.step(2.0, lambda rows: matmul(rows, w_out, 1, 1), grad_branch)
    settle_out.cross()
    order.fill(order.clock)
    grad_w_out = DpSum(
        order, order.step(2.0, lambda a, b: matmul(a, b, 0, 0), attended, grad_branch), 0
    )
    heads = []
    for head in range(kv_heads):
        out, head_q_gain, head_k_gain = order.step(
            12.5,
            lambda grad: attend_back(
                head, lengths, query, key, value, attended, grad, raw_q, raw_k,
                q_gain, k_gain, cosine, sine,
            ),
            grad_attended,
        )
        grad_weights = DpSum(
            order, order.step(2.0, lambda a, b: matmul(a, b, 0, 0), whole_a, out), head % 2
        )
        heads.append((out, grad_weights, head_q_gain[0], head_k_gain[0]))
        order.fill(order.clock)
    grad_normed_a = order.step(
        3.0,
        lambda outs: sum(
            dot(out, weights, 1, 1) for out, weights in zip(outs, head_weights)
        ).astype(jnp.bfloat16),
        [one[0] for one in heads],
    )
    settle_a = Settle(order, grad_normed_a)
    settle_a.cross()
    layer_out = jnp.where(live_rows, mixed + settle_out.land(), 0.0)
    _, attn_norm_back = jax.vjp(rms_norm, resid, attn_gain)
    grad_resid_norm, grad_attn_gain = attn_norm_back(settle_a.land())
    tokens_grad = grad_mixed + grad_resid_norm
    gains = GainSum(
        order,
        jnp.concatenate(
            [
                grad_attn_gain,
                grad_mlp_gain,
                sum(one[2] for one in heads),
                sum(one[3] for one in heads),
            ]
        ),
    )
    order.finish()

    width = attn_gain.shape[0]
    grad_attn_gain, grad_mlp_gain, grad_q_gain, grad_k_gain = jnp.split(
        gains.part, [width, 2 * width, 2 * width + HEAD_SIZE]
    )
    by_head = [one[1].part.astype(jnp.float32) for one in heads]
    value_col = group_cols + HEAD_SIZE
    return (
        layer_out,
        tokens_grad,
        grad_attn_gain,
        grad_q_gain,
        grad_k_gain,
        grad_mlp_gain,
        jnp.concatenate([one[:, :group_cols] for one in by_head], axis=1),
        jnp.concatenate([one[:, group_cols:value_col] for one in by_head], axis=1),
        jnp.concatenate([one[:, value_col:] for one in by_head], axis=1),
        grad_w_out.part.astype(jnp.float32),
        grad_w_gate.part.astype(jnp.float32),
        grad_w_up.part.astype(jnp.float32),
        grad_w_down.part.astype(jnp.float32),
    )


def solution(mesh):
    return jax.shard_map(
        body,
        mesh=mesh,
        in_specs=(
            P(("dp", "tensor"), None),
            P(("dp", "tensor"), None),
            P(),
            P(),
            P(),
            P(),
            P(None, "tensor"),
            P(None, "tensor"),
            P(None, "tensor"),
            P("tensor", None),
            P(None, "tensor"),
            P(None, "tensor"),
            P("tensor", None),
            P("dp"),
        ),
        out_specs=(
            P(("dp", "tensor"), None),
            P(("dp", "tensor"), None),
            P(),
            P(),
            P(),
            P(),
            P(None, "tensor"),
            P(None, "tensor"),
            P(None, "tensor"),
            P("tensor", None),
            P(None, "tensor"),
            P(None, "tensor"),
            P("tensor", None),
        ),
        check_vma=False,
    )
```

```python
import jax
import jax.numpy as jnp
from jax import lax
from jax.experimental import pallas as pl
from jax.experimental.pallas import tpu as pltpu
from jax.sharding import PartitionSpec as P

HEAD_SIZE = 128
BLOCK_ROWS = 256
epsilon = 1e-06
rotary_base = 1000000.0


def rotary_tables(every_row):
    half_width = HEAD_SIZE // 2
    frequency = rotary_base ** (-(jnp.arange(half_width, dtype=jnp.float32) * 2.0) / HEAD_SIZE)
    angles = jnp.arange(every_row, dtype=jnp.float32)[:, None] * frequency[None, :]
    cosine = jnp.cos(angles)
    sine = jnp.sin(angles)
    return (
        jnp.concatenate([cosine, cosine], axis=-1),
        jnp.concatenate([-sine, sine], axis=-1),
    )


def turned(values):
    return pltpu.roll(values, HEAD_SIZE // 2, 1)


def shaped(raw, gain, cosine, sine):
    normed = raw * lax.rsqrt(jnp.mean(raw * raw, axis=-1, keepdims=True) + epsilon) * gain
    return normed * cosine + turned(normed) * sine


def shaped_back(grad, raw, gain, cosine, sine):
    factor = lax.rsqrt(jnp.mean(raw * raw, axis=-1, keepdims=True) + epsilon)
    unit = raw * factor
    grad_normed = grad * cosine - turned(grad) * sine
    grad_gain = jnp.sum(grad_normed * unit, axis=0, keepdims=True)
    scaled = grad_normed * gain
    grad_raw = factor * (scaled - unit * jnp.mean(scaled * unit, axis=-1, keepdims=True))
    return grad_raw, grad_gain


def dot(left, right, left_dim, right_dim):
    return lax.dot_general(
        left, right, (((left_dim,), (right_dim,)), ((), ())), preferred_element_type=jnp.float32
    )


def heads_kernel(
    place_ref, mine_ref, near_ref, across_ref, far_ref, wq_ref, wk_ref, wv_ref, q_gain_ref, k_gain_ref, cos_ref, sin_ref,
    rows_ref, raw_q_ref, raw_k_ref, query_ref, key_ref, value_ref,
):
    for k, piece_ref in enumerate((mine_ref, near_ref, across_ref, far_ref)):

        @pl.when(pl.program_id(0) == k)
        def _():
            rows_ref[...] = piece_ref[...]

    rows = rows_ref[...]
    cosine = cos_ref[...]
    sine = sin_ref[...]
    value_ref[...] = dot(rows, wv_ref[...], 1, 0).astype(jnp.bfloat16)
    for weight_ref, gain_ref, raw_ref, out_ref in (
        (wq_ref, q_gain_ref, raw_q_ref, query_ref),
        (wk_ref, k_gain_ref, raw_k_ref, key_ref),
    ):
        raw = dot(rows, weight_ref[...], 1, 0)
        raw_ref[...] = raw
        for head in range(raw.shape[1] // HEAD_SIZE):
            cut = slice(head * HEAD_SIZE, (head + 1) * HEAD_SIZE)
            out_ref[:, cut] = shaped(raw[:, cut], gain_ref[...], cosine, sine).astype(jnp.bfloat16)


def project_heads(places, pieces, w_query, key_weight, value_weight, q_gain, k_gain, cosine, sine):
    block, width = pieces[0].shape
    every_row = block * len(pieces)
    q_cols, k_cols = w_query.shape[1], key_weight.shape[1]

    def by_row(cols):
        return pl.BlockSpec((block, cols), lambda i, places: (places[i], 0))

    def whole(shape):
        return pl.BlockSpec(shape, lambda i, places: (0, 0))

    outs = [
        (width, jnp.bfloat16), (q_cols, jnp.float32), (k_cols, jnp.float32),
        (q_cols, jnp.bfloat16), (k_cols, jnp.bfloat16), (k_cols, jnp.bfloat16),
    ]
    return pl.pallas_call(
        heads_kernel,
        grid_spec=pltpu.PrefetchScalarGridSpec(
            num_scalar_prefetch=1,
            grid=(len(pieces),),
            in_specs=[whole(one.shape) for one in pieces]
            + [
                whole(w_query.shape),
                whole(key_weight.shape),
                whole(value_weight.shape),
                whole((1, HEAD_SIZE)),
                whole((1, HEAD_SIZE)),
                by_row(HEAD_SIZE),
                by_row(HEAD_SIZE),
            ],
            out_specs=[by_row(cols) for cols, _ in outs],
        ),
        out_shape=[jax.ShapeDtypeStruct((every_row, cols), kind) for cols, kind in outs],
        name="project_heads",
    )(
        places, *pieces, w_query, key_weight, value_weight,
        q_gain.reshape(1, HEAD_SIZE), k_gain.reshape(1, HEAD_SIZE), cosine, sine,
    )


def live_lanes(length, every_row):
    row = lax.broadcasted_iota(jnp.int32, (every_row, HEAD_SIZE), 0)
    return jnp.where(row < length, 1.0, 0.0)


def exponents(query, key, diagonal):
    raised = jnp.exp2(dot(query, key, 1, 1) * (HEAD_SIZE ** (-0.5) * 1.4426950408889634))
    if diagonal:
        row = lax.broadcasted_iota(jnp.int32, raised.shape, 0)
        place = lax.broadcasted_iota(jnp.int32, raised.shape, 1)
        raised = jnp.where(place <= row, raised, 0.0)
    return raised


def spans(first_row):
    whole = [(slice(0, first_row), False)] if first_row else []
    return whole + [(slice(first_row, first_row + BLOCK_ROWS), True)]


def attend_kernel(length_ref, query_ref, key_ref, value_ref, out_ref):
    every_row = key_ref.shape[0]
    live = live_lanes(length_ref[0], every_row)
    values = jnp.concatenate(
        [(value_ref[...].astype(jnp.float32) * live).astype(jnp.bfloat16), live.astype(jnp.bfloat16)],
        axis=1,
    )
    for first_row in range(0, every_row, BLOCK_ROWS):
        rows = slice(first_row, first_row + BLOCK_ROWS)
        total = 0.0
        for span, diagonal in spans(first_row):
            raised = exponents(query_ref[rows, :], key_ref[span, :], diagonal)
            total = total + dot(raised.astype(jnp.bfloat16), values[span], 1, 0)
        out_ref[rows, :] = (total[:, :HEAD_SIZE] / total[:, HEAD_SIZE:]).astype(jnp.bfloat16)


def attend(lengths, query, key, value):
    every_row, q_cols = query.shape
    group = q_cols // key.shape[1]

    def head_spec(share):
        return pl.BlockSpec((every_row, HEAD_SIZE), lambda h, lengths: (0, h // share))

    return pl.pallas_call(
        attend_kernel,
        grid_spec=pltpu.PrefetchScalarGridSpec(
            num_scalar_prefetch=1,
            grid=(q_cols // HEAD_SIZE,),
            in_specs=[head_spec(1), head_spec(group), head_spec(group)],
            out_specs=head_spec(1),
        ),
        out_shape=jax.ShapeDtypeStruct((every_row, q_cols), jnp.bfloat16),
        name="attend",
    )(lengths, query, key, value)


def attend_back_kernel(
    length_ref, query_ref, key_ref, value_ref, attended_ref, grad_ref, raw_q_ref, raw_k_ref,
    q_gain_ref, k_gain_ref, cos_ref, sin_ref,
    out_ref, gain_q_ref, gain_k_ref,
    key_acc, value_acc,
):
    every_row = key_ref.shape[0]
    group = query_ref.shape[1] // HEAD_SIZE
    scaling = HEAD_SIZE ** (-0.5)
    live = live_lanes(length_ref[0], every_row)
    ones = live.astype(jnp.bfloat16)
    keys = (key_ref[...].astype(jnp.float32) * live).astype(jnp.bfloat16)
    key_acc[...] = jnp.zeros_like(key_acc)
    value_acc[...] = jnp.zeros_like(value_acc)
    gain_q = jnp.zeros((1, HEAD_SIZE), jnp.float32)
    for head in range(group):
        cut = slice(head * HEAD_SIZE, (head + 1) * HEAD_SIZE)
        for first_row in range(0, every_row, BLOCK_ROWS):
            rows = slice(first_row, first_row + BLOCK_ROWS)
            query = query_ref[rows, cut]
            grad = grad_ref[rows, cut]
            grad_wide = grad.astype(jnp.float32)
            delta = jnp.sum(
                grad_wide * attended_ref[rows, cut].astype(jnp.float32), axis=-1, keepdims=True
            )
            sums = 0.0
            grad_query = 0.0
            parts = []
            for span, diagonal in spans(first_row):
                raised = exponents(query, key_ref[span, :], diagonal)
                grad_scores = raised * (dot(grad, value_ref[span, :], 1, 1) - delta)
                raised = raised.astype(jnp.bfloat16)
                grad_scores = grad_scores.astype(jnp.bfloat16)
                sums = sums + dot(raised, ones[span], 1, 0)
                grad_query = grad_query + dot(grad_scores, keys[span], 1, 0)
                parts.append((span, raised, grad_scores))
            inverse = 1.0 / sums
            query_share = (query.astype(jnp.float32) * inverse).astype(jnp.bfloat16)
            grad_share = (grad_wide * inverse).astype(jnp.bfloat16)
            for span, raised, grad_scores in parts:
                key_acc[span, :] += dot(grad_scores, query_share, 0, 0)
                value_acc[span, :] += dot(raised, grad_share, 0, 0)
            grad_raw, grad_gain = shaped_back(
                grad_query * (inverse * scaling), raw_q_ref[rows, cut], q_gain_ref[...],
                cos_ref[rows, :], sin_ref[rows, :],
            )
            out_ref[rows, cut] = grad_raw.astype(jnp.bfloat16)
            gain_q += grad_gain
    gain_q_ref[...] = gain_q
    grad_raw, grad_gain = shaped_back(
        key_acc[...] * (live * scaling), raw_k_ref[...], k_gain_ref[...], cos_ref[...], sin_ref[...]
    )
    key_col = group * HEAD_SIZE
    value_col = key_col + HEAD_SIZE
    out_ref[:, key_col:value_col] = grad_raw.astype(jnp.bfloat16)
    out_ref[:, value_col:] = (value_acc[...] * live).astype(jnp.bfloat16)
    gain_k_ref[...] = grad_gain


def attend_back(
    kv_head, lengths, query, key, value, attended, grad, raw_q, raw_k, q_gain, k_gain, cosine, sine
):
    every_row, q_cols = query.shape
    group_cols = q_cols // key.shape[1] * HEAD_SIZE

    def cut(cols):
        return pl.BlockSpec((every_row, cols), lambda i, lengths: (0, kv_head))

    def whole(rows, cols):
        return pl.BlockSpec((rows, cols), lambda i, lengths: (0, 0))

    return pl.pallas_call(
        attend_back_kernel,
        grid_spec=pltpu.PrefetchScalarGridSpec(
            num_scalar_prefetch=1,
            grid=(1,),
            in_specs=[
                cut(group_cols), cut(HEAD_SIZE), cut(HEAD_SIZE), cut(group_cols),
                cut(group_cols), cut(group_cols), cut(HEAD_SIZE),
                whole(1, HEAD_SIZE), whole(1, HEAD_SIZE),
                whole(every_row, HEAD_SIZE), whole(every_row, HEAD_SIZE),
            ],
            out_specs=[
                whole(every_row, group_cols + 2 * HEAD_SIZE),
                whole(1, HEAD_SIZE), whole(1, HEAD_SIZE),
            ],
            scratch_shapes=[
                pltpu.VMEM((every_row, HEAD_SIZE), jnp.float32),
                pltpu.VMEM((every_row, HEAD_SIZE), jnp.float32),
            ],
        ),
        out_shape=[
            jax.ShapeDtypeStruct((every_row, group_cols + 2 * HEAD_SIZE), jnp.bfloat16),
            jax.ShapeDtypeStruct((1, HEAD_SIZE), jnp.float32),
            jax.ShapeDtypeStruct((1, HEAD_SIZE), jnp.float32),
        ],
        name="attend_back",
    )(
        lengths, query, key, value, attended, grad, raw_q, raw_k,
        q_gain.reshape(1, HEAD_SIZE), k_gain.reshape(1, HEAD_SIZE), cosine, sine,
    )


def rows_at(block, rows):
    return pl.ds(pl.multiple_of(block * rows, rows), rows)


def join_kernel(place_ref, *refs):
    for k, piece_ref in enumerate(refs[:-1]):
        rows = piece_ref.shape[0]
        refs[-1][rows_at(place_ref[k], rows), :] = piece_ref[...].astype(refs[-1].dtype)


def in_vmem(count):
    return [pl.BlockSpec(memory_space=pltpu.VMEM)] * count


def join(places, pieces, dtype=jnp.bfloat16):
    rows, width = pieces[0].shape
    count = len(pieces)
    if rows % 16:
        return jnp.stack(pieces)[jnp.argsort(places)].reshape(count * rows, width).astype(dtype)
    return pl.pallas_call(
        join_kernel,
        in_specs=[pl.BlockSpec(memory_space=pltpu.SMEM)] + in_vmem(count),
        out_specs=in_vmem(1)[0],
        out_shape=jax.ShapeDtypeStruct((count * rows, width), dtype),
        name="join",
    )(places, *pieces)


def rms_norm(values, gain):
    return values * lax.rsqrt(jnp.mean(values * values, axis=-1, keepdims=True) + epsilon) * gain


def swiglu(gate_proj, up_proj):
    return gate_proj / (1.0 + jnp.exp(-gate_proj)) * up_proj


def matmul(left, right, left_dim, right_dim):
    return dot(left, right, left_dim, right_dim).astype(jnp.bfloat16)


def bit_of(axis, bit):
    return (lax.axis_index(axis) >> bit) & 1


def swap(values, axis, bit):
    size = lax.axis_size(axis)
    return lax.ppermute(values, axis, [(i, i ^ (1 << bit)) for i in range(size)])


def bits(axis):
    return list(range((lax.axis_size(axis) - 1).bit_length()))


def ordered_pair(mine, other, flag):
    is_first = flag == 0
    return jnp.concatenate(
        [jnp.where(is_first, mine, other), jnp.where(is_first, other, mine)], axis=0
    )


def halves(values, flag):
    rows = values.shape[0] // 2
    sent = lax.dynamic_slice_in_dim(values, (1 - flag) * rows, rows, 0)
    kept = lax.dynamic_slice_in_dim(values, flag * rows, rows, 0)
    return sent, kept


def after(values, done):
    return lax.optimization_barrier((values, done))[0]


class Flight:
    def __init__(self, received, arrival):
        self.received = received
        self.arrival = arrival


class Order:
    def __init__(self):
        self.clock = 0.0
        self.token = None
        self.free = {}
        self.sums = []

    def gate(self, values):
        return values if self.token is None else after(values, self.token)

    def step(self, us, function, *inputs):
        out = function(*self.gate(inputs))
        self.token = out
        self.clock += us
        return out

    def send(self, values, axis, bit):
        size = values.size * values.dtype.itemsize
        if axis == "tensor" and bit == 0:
            us = size / 400e3
        else:
            us = 2 * size / 75e3 * (2 if axis == "dp" and bit > 1 else 1)
        values = self.gate(values)
        received = swap(values, axis, bit)
        self.token = values
        self.clock += 1.6
        start = max(self.clock, self.free.get((axis, bit), 0.0))
        self.free[axis, bit] = start + us
        return Flight(received, start + us + 2.0)

    def fill(self, until):
        while True:
            waiting = [one for one in self.sums if one.flight is not None]
            if not waiting:
                break
            one = min(waiting, key=lambda one: one.flight.arrival)
            if one.flight.arrival > max(self.clock, until - 3.0):
                break
            self.clock = max(self.clock, one.flight.arrival)
            one.advance()

    def land(self, flight):
        self.fill(flight.arrival)
        self.clock = max(self.clock, flight.arrival)
        received = self.gate(flight.received)
        self.token = received
        return received

    def finish(self):
        self.fill(float("inf"))


class DpSum:
    def __init__(self, order, values, first):
        turns = bits("dp")
        self.order = order
        self.turns = turns[first:] + turns[:first]
        self.stage = 0
        self.rows = values.shape[0]
        self.terms = [(values, 0)]
        order.sums.append(self)
        self.launch()

    def total(self, start):
        parts = [
            lax.dynamic_slice_in_dim(values, first + start, self.rows, 0).astype(jnp.float32)
            for values, first in self.terms
        ]
        return sum(parts[1:], parts[0]).astype(jnp.bfloat16)

    def launch(self):
        count = len(self.turns)
        if self.stage < count:
            bit = self.turns[self.stage]
            self.rows //= 2
            flag = bit_of("dp", bit)
            sent = self.total((1 - flag) * self.rows)
            self.terms = [(values, first + flag * self.rows) for values, first in self.terms]
        else:
            bit = self.turns[2 * count - 1 - self.stage]
            if self.stage == count:
                self.part = self.total(0)
            sent = self.part
        self.order.clock += 0.8
        self.flight = self.order.send(sent, "dp", bit)

    def advance(self):
        count = len(self.turns)
        received = self.order.gate(self.flight.received)
        self.order.token = received
        self.stage += 1
        if self.stage <= count:
            self.terms = self.terms + [(received, 0)]
        else:
            self.flag = bit_of("dp", self.turns[2 * count - self.stage])
            self.last = (self.part, received)
            self.part = ordered_pair(*self.last, self.flag)
            self.order.token = self.part
            self.order.clock += 1.0
            if self.stage == 2 * count:
                self.flight = None
                return
        self.launch()


class GainSum:
    def __init__(self, order, values):
        self.order = order
        self.part = values
        self.turns = [(axis, bit) for axis in ("tensor", "dp") for bit in bits(axis)]
        order.sums.append(self)
        self.launch()

    def launch(self):
        self.flight = self.order.send(self.part, *self.turns.pop(0)) if self.turns else None
        if self.flight is not None:
            self.flight.arrival += 12.0

    def advance(self):
        self.part = self.part + self.order.gate(self.flight.received)
        self.order.token = self.part
        self.launch()


class Spread:
    def __init__(self, order, values):
        self.order = order
        self.values = values
        self.across = order.send(values, "tensor", 1)
        self.near = order.send(values, "tensor", 0)

    def pieces(self):
        across = self.order.land(self.across)
        far = self.order.send(across, "tensor", 0)
        near = self.order.gate(self.near.received)
        return [self.values, near, across, far.received]

    def land(self, places):
        return self.order.step(2.0, lambda *pieces: join(places, pieces), *self.pieces())


class Settle:
    def __init__(self, order, values):
        self.order = order
        core = bit_of("tensor", 0)
        rows = values.shape[0] // 4
        parts = values.reshape(2, 2, rows, values.shape[1])
        sent = lax.dynamic_slice_in_dim(parts, 1 - core, 1, 1)
        self.kept = lax.dynamic_slice_in_dim(parts, core, 1, 1)
        self.flight = order.send(sent, "tensor", 0)

    def cross(self):
        side = bit_of("tensor", 1)
        received = self.order.land(self.flight)
        pair = (self.kept.astype(jnp.float32) + received.astype(jnp.float32))[:, 0]
        away = lax.dynamic_slice_in_dim(pair, 1 - side, 1, 0)[0].astype(jnp.bfloat16)
        self.home = lax.dynamic_slice_in_dim(pair, side, 1, 0)[0]
        self.order.clock += 2.0
        self.flight = self.order.send(away, "tensor", 1)

    def land(self):
        return self.home + self.order.land(self.flight).astype(jnp.float32)


class SettlePieces:
    def __init__(self, order, us, function, near_far, mine_across):
        self.order = order
        self.flight = order.send(order.step(us, function, near_far), "tensor", 0)
        self.kept = order.step(us, function, mine_across)

    def cross(self):
        self.near = self.order.land(self.flight)
        rows = self.near.shape[0] // 2
        self.order.clock += 1.0
        away = self.kept[rows:].astype(jnp.float32) + self.near[rows:].astype(jnp.float32)
        self.flight = self.order.send(away.astype(jnp.bfloat16), "tensor", 1)

    def land(self):
        received = self.order.land(self.flight).astype(jnp.float32)
        kept, near = after((self.kept, self.near), received)
        rows = near.shape[0] // 2
        return kept[:rows].astype(jnp.float32) + near[:rows].astype(jnp.float32) + received


def body(
    tokens,
    cotangent,
    attn_gain,
    q_gain,
    k_gain,
    mlp_gain,
    w_query,
    key_weight,
    value_weight,
    w_out,
    w_gate,
    w_up,
    w_down,
    lengths,
):
    share_rows = tokens.shape[0]
    every_row = share_rows * lax.axis_size("tensor")
    kv_heads = key_weight.shape[1] // HEAD_SIZE
    group_cols = w_query.shape[1] // kv_heads
    length = lengths[0]
    first_row = lax.axis_index("tensor") * share_rows
    live_rows = (first_row + jnp.arange(share_rows, dtype=jnp.int32) < length)[:, None]
    order = Order()

    core = bit_of("tensor", 0)
    side = bit_of("tensor", 1)
    turn = jnp.arange(4, dtype=jnp.int32)
    places = (side ^ (turn >> 1)) * 2 + (core ^ (turn & 1))

    resid = tokens.astype(jnp.float32)
    gather_a = Spread(order, rms_norm(resid, attn_gain).astype(jnp.bfloat16))
    cosine, sine = rotary_tables(every_row)
    grad_out = jnp.where(live_rows, cotangent.astype(jnp.float32), 0.0)
    head_weights = [
        jnp.concatenate(
            [
                w_query[:, head * group_cols : (head + 1) * group_cols],
                key_weight[:, head * HEAD_SIZE : (head + 1) * HEAD_SIZE],
                value_weight[:, head * HEAD_SIZE : (head + 1) * HEAD_SIZE],
            ],
            axis=1,
        )
        for head in range(kv_heads)
    ]
    pieces_a = gather_a.pieces()
    gather_ffn = Spread(order, grad_out.astype(jnp.bfloat16))
    whole_a, raw_q, raw_k, query, key, value = order.step(
        7.5,
        lambda *pieces: project_heads(
            places, pieces, w_query, key_weight, value_weight, q_gain, k_gain, cosine, sine
        ),
        *pieces_a,
    )
    attended = order.step(
        11.0, lambda query, key, value: attend(lengths, query, key, value), query, key, value
    )
    whole_ffn = jnp.concatenate(gather_ffn.pieces(), axis=0)
    branch_out = order.step(1.5, lambda rows: matmul(rows, w_out, 1, 0), attended)
    settle_mixed = Settle(order, branch_out)
    settle_mixed.cross()
    grad_act = order.step(2.0, lambda rows: matmul(rows, w_down, 1, 1), whole_ffn)
    mixed = resid + settle_mixed.land()

    order.clock += 2.0
    gather_m = Spread(order, rms_norm(mixed, mlp_gain).astype(jnp.bfloat16))

    def hidden(rows, grad_act):
        gate_proj = dot(rows, w_gate, 1, 0)
        up_proj = dot(rows, w_up, 1, 0)
        activated, swiglu_back = jax.vjp(swiglu, gate_proj, up_proj)
        grad_gate, grad_up = swiglu_back(grad_act.astype(jnp.float32))
        return (
            activated.astype(jnp.bfloat16),
            grad_gate.astype(jnp.bfloat16),
            grad_up.astype(jnp.bfloat16),
        )

    near_m = jnp.concatenate([gather_m.values, gather_m.near.received], axis=0)
    half = near_m.shape[0]
    near_hidden = order.step(4.0, hidden, near_m, grad_act[:half])
    far_m = jnp.concatenate(gather_m.pieces()[2:], axis=0)
    far_hidden = order.step(4.0, hidden, far_m, grad_act[half:])
    whole_m = jnp.concatenate([near_m, far_m], axis=0)
    activated, grad_gate, grad_up = [
        jnp.concatenate(both, axis=0) for both in zip(near_hidden, far_hidden)
    ]
    quarter = half // 2
    near_far = [
        jnp.concatenate([near[quarter:], far[quarter:]], axis=0)
        for near, far in zip(near_hidden, far_hidden)
    ]
    mine_across = [
        jnp.concatenate([near[:quarter], far[:quarter]], axis=0)
        for near, far in zip(near_hidden, far_hidden)
    ]
    grad_w_down = DpSum(
        order, order.step(2.0, lambda a, b: matmul(a, b, 0, 0), activated, whole_ffn), 0
    )
    grad_normed_m = order.step(
        4.0,
        lambda a, b: (dot(a, w_gate, 1, 1) + dot(b, w_up, 1, 1)).astype(jnp.bfloat16),
        grad_gate, grad_up,
    )
    settle_m = SettlePieces(
        order, 2.0,
        lambda grads: (dot(grads[1], w_gate, 1, 1) + dot(grads[2], w_up, 1, 1)).astype(jnp.bfloat16),
        near_far, mine_across,
    )
    settle_m.cross()
    grad_w_gate = DpSum(
        order, order.step(2.0, lambda a, b: matmul(a, b, 0, 0), whole_m, grad_gate), 0
    )
    up_grad = order.step(2.0, lambda a, b: matmul(a, b, 0, 0), whole_m, grad_up)
    _, mlp_norm_back = jax.vjp(rms_norm, mixed, mlp_gain)
    grad_mixed_norm, grad_mlp_gain = mlp_norm_back(settle_m.land())
    grad_mixed = grad_out + grad_mixed_norm
    order.clock += 2.0
    gather_branch = Spread(order, grad_mixed.astype(jnp.bfloat16))
    grad_w_up = DpSum(order, up_grad, 0)
    settle_out = SettlePieces(
        order, 1.5, lambda rows: matmul(rows[0], w_down, 1, 0), near_far, mine_across
    )
    grad_branch = gather_branch.land(places)

    grad_attended = order.step(2.0, lambda rows: matmul(rows, w_out, 1, 1), grad_branch)
    settle_out.cross()
    order.fill(order.clock)
    grad_w_out = DpSum(
        order, order.step(2.0, lambda a, b: matmul(a, b, 0, 0), attended, grad_branch), 0
    )
    heads = []
    for head in range(kv_heads):
        out, head_q_gain, head_k_gain = order.step(
            12.5,
            lambda grad: attend_back(
                head, lengths, query, key, value, attended, grad, raw_q, raw_k,
                q_gain, k_gain, cosine, sine,
            ),
            grad_attended,
        )
        grad_weights = DpSum(
            order, order.step(2.0, lambda a, b: matmul(a, b, 0, 0), whole_a, out), head % 2
        )
        heads.append((out, grad_weights, head_q_gain[0], head_k_gain[0]))
        order.fill(order.clock)
    grad_normed_a = order.step(
        3.0,
        lambda outs: sum(
            dot(out, weights, 1, 1) for out, weights in zip(outs, head_weights)
        ).astype(jnp.bfloat16),
        [one[0] for one in heads],
    )
    settle_a = Settle(order, grad_normed_a)
    settle_a.cross()
    layer_out = jnp.where(live_rows, mixed + settle_out.land(), 0.0)
    _, attn_norm_back = jax.vjp(rms_norm, resid, attn_gain)
    grad_resid_norm, grad_attn_gain = attn_norm_back(settle_a.land())
    tokens_grad = grad_mixed + grad_resid_norm
    gains = GainSum(
        order,
        jnp.concatenate(
            [
                grad_attn_gain,
                grad_mlp_gain,
                sum(one[2] for one in heads),
                sum(one[3] for one in heads),
            ]
        ),
    )
    order.finish()

    width = attn_gain.shape[0]
    grad_attn_gain, grad_mlp_gain, grad_q_gain, grad_k_gain = jnp.split(
        gains.part, [width, 2 * width, 2 * width + HEAD_SIZE]
    )
    by_head = [one[1].part.astype(jnp.float32) for one in heads]
    value_col = group_cols + HEAD_SIZE
    return (
        layer_out,
        tokens_grad,
        grad_attn_gain,
        grad_q_gain,
        grad_k_gain,
        grad_mlp_gain,
        jnp.concatenate([one[:, :group_cols] for one in by_head], axis=1),
        jnp.concatenate([one[:, group_cols:value_col] for one in by_head], axis=1),
        jnp.concatenate([one[:, value_col:] for one in by_head], axis=1),
        grad_w_out.part.astype(jnp.float32),
        grad_w_gate.part.astype(jnp.float32),
        grad_w_up.part.astype(jnp.float32),
        grad_w_down.part.astype(jnp.float32),
    )


def solution(mesh):
    return jax.shard_map(
        body,
        mesh=mesh,
        in_specs=(
            P(("dp", "tensor"), None),
            P(("dp", "tensor"), None),
            P(),
            P(),
            P(),
            P(),
            P(None, "tensor"),
            P(None, "tensor"),
            P(None, "tensor"),
            P("tensor", None),
            P(None, "tensor"),
            P(None, "tensor"),
            P("tensor", None),
            P("dp"),
        ),
        out_specs=(
            P(("dp", "tensor"), None),
            P(("dp", "tensor"), None),
            P(),
            P(),
            P(),
            P(),
            P(None, "tensor"),
            P(None, "tensor"),
            P(None, "tensor"),
            P("tensor", None),
            P(None, "tensor"),
            P(None, "tensor"),
            P("tensor", None),
        ),
        check_vma=False,
    )
```
